32 devices in a mesh: dp: 4 (over y, x), fsdp: 8 (over z, core).
Axes of the slice: x: 2, y: 2, z: 4, core: 2. Of those that a mesh axis runs over, the one named last changes fastest.
Arguments:
- molecules: bfloat16 [32, 512, 768], P(('dp', 'fsdp')), may hold values from -6 to 6
- seq_lengths: int32 [32], P(('dp', 'fsdp')), may hold values from 461 to 512
- hash_ids: int32 [8, 65536], P(None, ('dp', 'fsdp')), may hold values from 0 to 16383
- out_grad: bfloat16 [32, 512, 768], P(('dp', 'fsdp')), may hold values from -6 to 6
- ln1_gain: bfloat16 [768], P(('dp', 'fsdp')), may hold values from 0.5 to 1.5
- ln1_bias: bfloat16 [768], P(('dp', 'fsdp')), may hold values from -0.625 to 0.625
- w_query: bfloat16 [768, 768], P(('dp', 'fsdp')), may hold values from -0.21875 to 0.21875
- b_query: bfloat16 [768], P(('dp', 'fsdp')), may hold values from -1.75 to 1.75
- w_key: bfloat16 [768, 768], P(('dp', 'fsdp')), may hold values from -0.21875 to 0.21875
- w_value: bfloat16 [768, 768], P(('dp', 'fsdp')), may hold values from -0.21875 to 0.21875
- b_value: bfloat16 [768], P(('dp', 'fsdp')), may hold values from -0.125 to 0.125
- w_out: bfloat16 [768, 768], P(('dp', 'fsdp')), may hold values from -3 to 3
- b_out: bfloat16 [768], P(('dp', 'fsdp')), may hold values from -0.625 to 0.625
- ln2_gain: bfloat16 [768], P(('dp', 'fsdp')), may hold values from 0.5 to 1.5
- ln2_bias: bfloat16 [768], P(('dp', 'fsdp')), may hold values from -0.625 to 0.625
- w_inner: bfloat16 [768, 3072], P(('dp', 'fsdp')), may hold values from -0.21875 to 0.21875
- b_inner: bfloat16 [3072], P(('dp', 'fsdp')), may hold values from -0.625 to 0.625
- w_outer: bfloat16 [3072, 768], P(('dp', 'fsdp')), may hold values from -0.109375 to 0.109375
- feedforward_output_bias: bfloat16 [768], P(('dp', 'fsdp')), may hold values from -0.625 to 0.625
Outputs:
- output: bfloat16 [32, 512, 768], P(('dp', 'fsdp'))
- in_grad: bfloat16 [32, 512, 768], P(('dp', 'fsdp'))
- grad_ln1_gain: float32 [768], P(('dp', 'fsdp'))
- grad_ln1_bias: float32 [768], P(('dp', 'fsdp'))
- grad_w_query: float32 [768, 768], P(('dp', 'fsdp'))
- grad_b_query: float32 [768], P(('dp', 'fsdp'))
- grad_w_key: float32 [768, 768], P(('dp', 'fsdp'))
- grad_w_value: float32 [768, 768], P(('dp', 'fsdp'))
- grad_b_value: float32 [768], P(('dp', 'fsdp'))
- grad_w_out: float32 [768, 768], P(('dp', 'fsdp'))
- grad_b_out: float32 [768], P(('dp', 'fsdp'))
- grad_ln2_gain: float32 [768], P(('dp', 'fsdp'))
- grad_ln2_bias: float32 [768], P(('dp', 'fsdp'))
- grad_w_inner: float32 [768, 3072], P(('dp', 'fsdp'))
- grad_b_inner: float32 [3072], P(('dp', 'fsdp'))
- grad_w_outer: float32 [3072, 768], P(('dp', 'fsdp'))
- grad_b_outer: float32 [768], P(('dp', 'fsdp'))
- counts: int32 [8, 16384], replicated
The draws below stay inside these ranges and needn't reach their ends.
All inputs are finite; a program needn't handle non-finite values.
Results may differ from the reference program's by a relative error of at most 0.013.
Values may be sent and summed in bfloat16 or wider, within the bound.
A program may use at most 192 MiB of HBM per device.

```python
import math
import jax
import jax.numpy as jnp
import numpy as np
from jax import lax

D = 768
HEADS = 12
HEAD_DIM = 64
FF = 3072
HASHES = 8
BUCKETS = 16384
SEQ_LEN = 512
SEQS = 32
CHARS = 65536


def draw_seq_lengths(key, part):
    lowest = SEQ_LEN - SEQ_LEN // 10
    lengths = jax.random.randint(jax.random.fold_in(key, 11), (SEQS,), lowest, SEQ_LEN + 1)
    first_slot = jax.random.randint(jax.random.fold_in(key, 12), (), 0, SEQS)
    offset = jax.random.randint(jax.random.fold_in(key, 13), (), 1, SEQS)
    lengths = lengths.at[first_slot].set(SEQ_LEN)
    lengths = lengths.at[(first_slot + offset) % SEQS].set(lowest)
    return lengths.astype(jnp.int32)


def place_ends(drawn, stream_key, least, top_value):
    dims = drawn.shape
    place = [jax.random.randint(jax.random.fold_in(stream_key, axis), (), 0, dims[axis]) for axis in range(len(dims))]
    drawn = drawn.at[tuple(place)].set(least)
    longest = dims.index(max(dims))
    place[longest] = (place[longest] + 1) % dims[longest]
    return drawn.at[tuple(place)].set(top_value)


def shard_levels(own_key, dims, cuts, low, top_value):
    factor_of, own = 1.0, jax.random.fold_in(own_key, 6)
    for dim, shards_of in cuts:
        draws = jnp.exp(jax.random.uniform(jax.random.fold_in(own, dim), (shards_of,), jnp.float32, low / len(cuts), top_value / len(cuts)))
        factor_of = factor_of * jnp.repeat(draws, dims[dim] // shards_of).reshape([-1 if axis == dim else 1 for axis in range(len(dims))])
    return factor_of


def rank_bounds(count, lean):
    loads = [(1 << 20) // math.isqrt(standing ** lean) + 1 for standing in range(1, count + 1)]
    scale = 1 + sum(loads) // (1 << 30)
    return np.cumsum(np.array([max(1, weight // scale) for weight in loads]))


def ranked(stream_key, dims, count, slope):
    listing = rank_bounds(count, slope)
    pick = jax.random.randint(jax.random.fold_in(stream_key, 1), dims, 0, int(listing[count - 1]))
    grade = jnp.searchsorted(jnp.asarray(listing, jnp.int32), pick, side="right")
    return jax.random.permutation(jax.random.fold_in(stream_key, 2), count)[grade].astype(jnp.int32)


def bell_draw(stream_key, shape, width, bound, split=(), held_as=jnp.bfloat16):
    level = shard_levels(stream_key, shape, split, -0.22, 0.18) if split else 1.0
    values = jax.random.normal(stream_key, shape, jnp.float32) * width * level
    return jnp.minimum(jnp.maximum(values, -bound), bound).astype(held_as)


def setup_inputs(seed: int = 0) -> dict:
    keys = jax.random.split(jax.random.key(seed), 20)
    molecules = bell_draw(keys[0], (SEQS, SEQ_LEN, D), 1.0, 6.0, ((0, 32),))
    seq_lengths = draw_seq_lengths(jax.random.fold_in(keys[19], 71), 0)
    hash_ids = place_ends(ranked(keys[2], (HASHES, CHARS), BUCKETS, 2), jax.random.fold_in(keys[2], 3), 0, BUCKETS - 1).astype(jnp.int32)
    out_grad = bell_draw(keys[3], (SEQS, SEQ_LEN, D), 1.0, 6.0, ((0, 32),))
    ln1_gain = jnp.clip(1.0 + 0.1 * jax.random.normal(keys[4], (D,), jnp.float32), 0.5, 1.5).astype(jnp.bfloat16)
    ln1_bias = bell_draw(keys[5], (D,), 0.1, 0.625, ((0, 32),))
    w_query = bell_draw(keys[6], (D, D), D ** -0.5, 0.21875, ((0, 32),))
    b_query = bell_draw(keys[7], (D,), 0.3, 1.75, ((0, 32),))
    w_key = bell_draw(keys[8], (D, D), D ** -0.5, 0.21875, ((0, 32),))
    w_value = bell_draw(keys[9], (D, D), D ** -0.5, 0.21875, ((0, 32),))
    b_value = bell_draw(keys[10], (D,), 0.02, 0.125, ((0, 32),))
    w_out = bell_draw(keys[11], (D, D), (max(1, 3 * D // SEQ_LEN)) ** -0.5, 3.0, ((0, 32),))
    b_out = bell_draw(keys[12], (D,), 0.1, 0.625, ((0, 32),))
    ln2_gain = jnp.clip(1.0 + 0.1 * jax.random.normal(keys[13], (D,), jnp.float32), 0.5, 1.5).astype(jnp.bfloat16)
    ln2_bias = bell_draw(keys[14], (D,), 0.1, 0.625, ((0, 32),))
    w_inner = bell_draw(keys[15], (D, FF), D ** -0.5, 0.21875, ((0, 32),))
    b_inner = bell_draw(keys[16], (FF,), 0.1, 0.625, ((0, 32),))
    w_outer = bell_draw(keys[17], (FF, D), FF ** -0.5, 0.109375, ((0, 32),))
    feedforward_output_bias = bell_draw(keys[18], (D,), 0.1, 0.625, ((0, 32),))
    return {"molecules": molecules, "seq_lengths": seq_lengths, "hash_ids": hash_ids, "out_grad": out_grad, "ln1_gain": ln1_gain, "ln1_bias": ln1_bias, "w_query": w_query, "b_query": b_query, "w_key": w_key, "w_value": w_value, "b_value": b_value, "w_out": w_out, "b_out": b_out, "ln2_gain": ln2_gain, "ln2_bias": ln2_bias, "w_inner": w_inner, "b_inner": b_inner, "w_outer": w_outer, "feedforward_output_bias": feedforward_output_bias}


HIGH = lax.Precision.HIGHEST
epsilon = 1e-05

@jax.custom_vjp
def low(v):
    return lax.optimization_barrier(v.astype(jnp.bfloat16)).astype(jnp.float32)

@jax.custom_vjp
def low_back(v):
    return v

def low_keep(v):
    return (low(v), None)

def low_pass(kept, grad):
    return (grad,)

def back_keep(v):
    return (v, None)

def back_low(kept, grad):
    return (low(grad),)
low.defvjp(low_keep, low_pass)
low_back.defvjp(back_keep, back_low)

def matmul_high(left, right):
    return jnp.dot(left, right, precision=HIGH, preferred_element_type=jnp.float32)

def norm_layer(values, gain, shift):
    center = values - lax.optimization_barrier(jnp.mean(values, axis=-1, keepdims=True))
    spread = lax.optimization_barrier(jnp.mean(center * center, axis=-1, keepdims=True))
    return center * lax.rsqrt(spread + epsilon) * gain + shift

def layer(sequence_rows, params, length):
    ln1_gain, ln1_bias, w_query, b_query, w_key, w_value, b_value, w_out, b_out, ln2_gain, ln2_bias, w_inner, b_inner, w_outer, feedforward_output_bias = params
    normed = low(norm_layer(sequence_rows, ln1_gain, ln1_bias))
    query_rows = low(low_back(matmul_high(normed, w_query)) + b_query)
    key_rows = low(low_back(matmul_high(normed, w_key)))
    value_rows = low(low_back(matmul_high(normed, w_value)) + b_value)
    head_shape = (SEQ_LEN, HEADS, HEAD_DIM)
    scores = jnp.einsum('qhd,khd->hqk', query_rows.reshape(head_shape), key_rows.reshape(head_shape), precision=HIGH) * HEAD_DIM ** (-0.5)
    key_mask = jnp.arange(SEQ_LEN) < length
    scores = low_back(jnp.where(key_mask[None, None, :], scores, -1e+30))
    probs = low(jax.nn.softmax(scores, axis=-1))
    context = jnp.einsum('hqk,khd->qhd', probs, value_rows.reshape(head_shape), precision=HIGH)
    context = low(low_back(context.reshape(SEQ_LEN, D)))
    middle = sequence_rows + (low_back(matmul_high(context, w_out)) + b_out)
    normed_two = low(norm_layer(middle, ln2_gain, ln2_bias))
    inner = low_back(matmul_high(normed_two, w_inner)) + b_inner
    hidden = low(jax.nn.gelu(inner, approximate=False))
    return middle + (low_back(matmul_high(hidden, w_outer)) + feedforward_output_bias)

def reference(molecules, seq_lengths, hash_ids, out_grad, ln1_gain, ln1_bias, w_query, b_query, w_key, w_value, b_value, w_out, b_out, ln2_gain, ln2_bias, w_inner, b_inner, w_outer, feedforward_output_bias):
    params = tuple((param.astype(jnp.float32) for param in (ln1_gain, ln1_bias, w_query, b_query, w_key, w_value, b_value, w_out, b_out, ln2_gain, ln2_bias, w_inner, b_inner, w_outer, feedforward_output_bias)))

    def one_sequence(totals, items):
        sequence_rows, length, seq_cotan = items

        def forward(rows_float, params_float):
            return layer(rows_float, params_float, length)
        result, pullback = jax.vjp(forward, sequence_rows.astype(jnp.float32), params)
        grad_rows, grad_params = pullback(seq_cotan.astype(jnp.float32))
        totals = tuple((total + grad for total, grad in zip(totals, grad_params)))
        return (totals, (result.astype(jnp.bfloat16), grad_rows.astype(jnp.bfloat16)))
    zeros = tuple((jnp.zeros(param.shape, jnp.float32) for param in params))
    totals, outputs = lax.scan(one_sequence, zeros, (molecules, seq_lengths, out_grad))
    output, in_grad = outputs
    table_rows = jnp.arange(HASHES, dtype=jnp.int32)[:, None]
    counts = jnp.zeros((HASHES, BUCKETS), jnp.int32).at[table_rows, hash_ids].add(1)
    return (output, in_grad, totals[0], totals[1], totals[2], totals[3], totals[4], totals[5], totals[6], totals[7], totals[8], totals[9], totals[10], totals[11], totals[12], totals[13], totals[14], counts)
```

```python
import functools

import jax
import jax.numpy as jnp
from jax import lax
from jax.experimental import pallas as pl
from jax.experimental.pallas import tpu as pltpu
from jax.sharding import PartitionSpec as P

F32=jnp.float32; BF=jnp.bfloat16
EPS=1e-5
RSQRT2=0.7071067811865476
RSQRT2PI=0.3989422804014327
LOG2E=1.4426950408889634
def mm(a,b): return lax.dot_general(a,b,(((1,),(0,)),((),())),preferred_element_type=F32)
def nt(a,b): return lax.dot_general(a,b,(((1,),(1,)),((),())),preferred_element_type=F32)
def tn(a,b): return lax.dot_general(a,b,(((0,),(0,)),((),())),preferred_element_type=F32)
def ds(i,n): return pl.ds(pl.multiple_of(i*n,n),n)
ROWT=128
def norm_rows(v):
    mean=jnp.mean(v,axis=-1,keepdims=True); cen=v-mean
    r=lax.rsqrt(jnp.mean(cen*cen,axis=-1,keepdims=True)+EPS)
    return cen*r, r
def ln1(r):
    g=r.sp[0:1,:]; b=r.sp[1:2,:]
    def body(i,_):
        n,_r=norm_rows(r.mol[ds(i,ROWT),:].astype(F32))
        r.nrm[ds(i,ROWT),:]=(n*g+b).astype(BF)
        return 0
    lax.fori_loop(0,512//ROWT,body,0)
CT=256
def qkv(r):
    D=768
    def body(j,_):
        n=r.nrm[...]
        q=mm(n,r.w1[:,ds(j,CT)])+r.sp[2:3,ds(j,CT)]
        r.q[:,ds(j,CT)]=(q.astype(BF).astype(F32)*0.125).astype(BF)
        r.k[:,ds(j,CT)]=mm(n,r.w1[:,ds(j+D//CT,CT)]).astype(BF)
        r.v[:,ds(j,CT)]=(mm(n,r.w1[:,ds(j+2*D//CT,CT)])+r.sp[3:4,ds(j,CT)]).astype(BF)
        return 0
    lax.fori_loop(0,D//CT,body,0)
def attn_pair_fwd(r,j,QT=512):
    lane=lax.broadcasted_iota(jnp.int32,(1,128),1); lo=lane<64
    kpos=lax.broadcasted_iota(jnp.int32,(512,128),0)
    bias=jnp.where(kpos<r.sl[0],0.0,-1e30/64).astype(BF)
    q2=r.q[:,ds(j,128)]; k2=r.k[:,ds(j,128)]; v2=r.v[:,ds(j,128)]
    one=jnp.ones((),BF)
    outs=[]
    for h in (0,1):
        half=lo if h==0 else jnp.logical_not(lo)
        qm=jnp.where(half,q2,one); km=jnp.where(half,k2,bias); vm=jnp.where(half,v2,one)
        s=nt(qm,km)
        m=jnp.max(s,axis=-1,keepdims=True)
        p=jnp.exp(s-m).astype(BF)
        r.p[2*j+h]=p
        outs.append(mm(p,vm))
    l=pltpu.roll(jnp.where(lo,outs[1],outs[0]),64,1)
    rl=1.0/l
    r.rl[:,ds(j,128)]=rl
    r.ctx[:,ds(j,128)]=(jnp.where(lo,outs[0],outs[1])*rl).astype(BF)
def attn_fwd(r):
    def body(j,_):
        attn_pair_fwd(r,j); return 0
    lax.fori_loop(0,6,body,0)
def outproj(r):
    def body(j,_):
        r.mid[:,ds(j,CT)]=r.mol[:,ds(j,CT)].astype(F32)+(mm(r.ctx[...],r.w1[:,ds(j+9,CT)])+r.sp[4:5,ds(j,CT)])
        return 0
    lax.fori_loop(0,3,body,0)
def ln2(r):
    g=r.sp[5:6,:]; b=r.sp[6:7,:]
    def body(i,_):
        n,_r=norm_rows(r.mid[ds(i,ROWT),:])
        v=n*g+b
        r.n2[ds(i,ROWT),:]=v.astype(BF)
        r.n2T[:,ds(i,ROWT)]=v.T.astype(BF)
        return 0
    lax.fori_loop(0,512//ROWT,body,0)
def inner(r):
    def body(j,_):
        u=mm(r.n2[...],r.wi[:,ds(j,CT)])+r.bi[0:1,ds(j,CT)]
        ph=0.5+0.5*lax.erf(u*RSQRT2)
        r.hid[:,ds(j,CT)]=(u*ph).astype(BF)
        r.gp[:,ds(j,CT)]=(ph+u*(RSQRT2PI*jnp.exp(-0.5*u*u))).astype(BF)
        return 0
    lax.fori_loop(0,3072//CT,body,0)
def gwu(r):
    def body(j,_):
        t=tn(r.hid[:,ds(j,CT)],r.og[...]).astype(BF)
        r.gu[0,ds(j,CT),:]=t[:,0:384]
        r.gu[1,ds(j,CT),:]=t[:,384:768]
        return 0
    lax.fori_loop(0,3072//CT,body,0)
    def body2(i,a): return a+jnp.sum(r.og[ds(i,ROWT),:].astype(F32),axis=0,keepdims=True)
    r.sg[7:8,:]=lax.fori_loop(0,512//ROWT,body2,jnp.zeros((1,768),F32))
def outp(r):
    def body(j,_):
        r.out[:,ds(j,CT)]=(r.mid[:,ds(j,CT)]+(mm(r.hid[...],r.wu[:,ds(j,CT)])+r.sp[7:8,ds(j,CT)])).astype(BF)
        return 0
    lax.fori_loop(0,3,body,0)
def ginner(r):
    def body(j,_):
        gi=nt(r.og[...],r.wu[ds(j,CT),:])*r.gp[:,ds(j,CT)].astype(F32)
        r.sgi[0:1,ds(j,CT)]=jnp.sum(gi,axis=0,keepdims=True)
        gib=gi.astype(BF)
        r.gil[:,ds(j,CT)]=gib
        r.gi[j//(1536//CT),:,ds(lax.rem(j,1536//CT),CT)]=mm(r.n2T[...],gib).astype(BF)
        return 0
    lax.fori_loop(0,3072//CT,body,0)
def gn2(r):
    def body(j,_):
        r.e[:,ds(j,CT)]=nt(r.gil[...],r.wi[ds(j,CT),:])
        return 0
    lax.fori_loop(0,3,body,0)
def ln_bwd(r,src,gain_row,base,first):
    gain=r.sp[gain_row:gain_row+1,:]
    def body(i,a):
        v=src[ds(i,ROWT),:].astype(F32)
        n,rs=norm_rows(v)
        e=r.e[ds(i,ROWT),:]
        eg=e*gain
        m1=jnp.mean(eg,axis=-1,keepdims=True); m2=jnp.mean(eg*n,axis=-1,keepdims=True)
        gv=rs*(eg-m1-n*m2)
        a0=a[0]+jnp.sum(e*n,axis=0,keepdims=True); a1=a[1]+jnp.sum(e,axis=0,keepdims=True)
        if first:
            r.ing[ds(i,ROWT),:]=(r.gm[ds(i,ROWT),:]+gv).astype(BF); return (a0,a1)
        gm=r.og[ds(i,ROWT),:].astype(F32)+gv
        r.gm[ds(i,ROWT),:]=gm; r.gml[ds(i,ROWT),:]=gm.astype(BF)
        return (a0,a1,a[2]+jnp.sum(gm,axis=0,keepdims=True))
    z=jnp.zeros((1,768),F32)
    return lax.fori_loop(0,512//ROWT,body,(z,z) if first else (z,z,z))
def ln2b(r):
    a=ln_bwd(r,r.mid,5,None,False)
    r.sg[5:6,:]=a[0]; r.sg[6:7,:]=a[1]; r.sg[4:5,:]=a[2]
def gctx(r):
    def body(j,_):
        r.gc[:,ds(j,CT)]=nt(r.gml[...],r.w1[ds(j,CT),2304:3072]).astype(BF)
        r.g1[1,ds(j,CT),768:1536]=tn(r.ctx[:,ds(j,CT)],r.gml[...]).astype(BF)
        return 0
    lax.fori_loop(0,3,body,0)
def attn_pair_bwd(r,j):
    lane=lax.broadcasted_iota(jnp.int32,(1,128),1); lo=lane<64
    q2=r.q[:,ds(j,128)]; k2=r.k[:,ds(j,128)]; v2=r.v[:,ds(j,128)]
    gp=r.gc[:,ds(j,128)].astype(F32)*r.rl[:,ds(j,128)]
    dd=r.ctx[:,ds(j,128)].astype(F32)*gp
    gpb=gp.astype(BF)
    zero=jnp.zeros((),BF)
    gT=gp.T.astype(BF); qT=q2.astype(F32).T.astype(BF)
    dq=[];dkT=[];dvT=[]
    for h in (0,1):
        half=lo if h==0 else jnp.logical_not(lo)
        D=jnp.sum(jnp.where(half,dd,0.0),axis=-1,keepdims=True)
        dp=nt(jnp.where(half,gpb,zero),v2)
        p=r.p[2*j+h]
        dsl=(p.astype(F32)*(dp-D)).astype(BF)
        dq.append(mm(dsl,k2))
        dvT.append(mm(gT[64*h:64*h+64],p))
        dkT.append(mm(qT[64*h:64*h+64],dsl))
    gq=jnp.where(lo,dq[0],dq[1])*0.125
    gv=jnp.concatenate(dvT,axis=0).T
    gk=jnp.concatenate(dkT,axis=0).T
    r.sg[2:3,ds(j,128)]=jnp.sum(gq,axis=0,keepdims=True)
    r.sg[3:4,ds(j,128)]=jnp.sum(gv,axis=0,keepdims=True)
    r.gq[:,ds(j,128)]=gq.astype(BF); r.gk[:,ds(j,128)]=gk.astype(BF); r.gv[:,ds(j,128)]=gv.astype(BF)
def attn_bwd(r):
    def body(j,_):
        attn_pair_bwd(r,j); return 0
    lax.fori_loop(0,6,body,0)
def gw1(r):
    def body(j,_):
        n=r.nrm[:,ds(j,CT)]
        r.g1[0,ds(j,CT),0:768]=tn(n,r.gq[...]).astype(BF)
        r.g1[0,ds(j,CT),768:1536]=tn(n,r.gk[...]).astype(BF)
        r.g1[1,ds(j,CT),0:768]=tn(n,r.gv[...]).astype(BF)
        return 0
    lax.fori_loop(0,3,body,0)
def gn1(r):
    def body(j,_):
        r.e[:,ds(j,CT)]=nt(r.gq[...],r.w1[ds(j,CT),0:768])+nt(r.gk[...],r.w1[ds(j,CT),768:1536])+nt(r.gv[...],r.w1[ds(j,CT),1536:2304])
        return 0
    lax.fori_loop(0,3,body,0)
def ln1b(r):
    a=ln_bwd(r,r.mol,0,None,True)
    r.sg[0:1,:]=a[0]; r.sg[1:2,:]=a[1]
PHASES=[ln1,qkv,attn_fwd,outproj,ln2,inner,gwu,outp,ginner,gn2,ln2b,gctx,attn_bwd,gw1,gn1,ln1b]
class NS: pass
INS=["sl","mol","og","sp","bi","w1","wi","wu"]
OUTS=[("out",(512,768),BF),("ing",(512,768),BF),("g1",(2,768,1536),BF),("gi",(2,768,1536),BF),("gu",(2,3072,384),BF),("sg",(8,768),F32),("sgi",(1,3072),F32)]
SCR=[("nrm",(512,768),BF),("q",(512,768),BF),("k",(512,768),BF),("v",(512,768),BF),("p",(12,512,512),BF),("rl",(512,768),F32),("ctx",(512,768),BF),
 ("mid",(512,768),F32),("n2",(512,768),BF),("n2T",(768,512),BF),("hid",(512,3072),BF),("gp",(512,3072),BF),("e",(512,768),F32),
 ("gc",(512,768),BF),]
ALIAS={"gil":"gp","gm":"mid","gml":"n2","gq":"gc","gk":"k","gv":"v"}
def kernel(phases,*refs):
    r=NS()
    names=INS+[o[0] for o in OUTS]+[s[0] for s in SCR]
    for n,x in zip(names,refs): setattr(r,n,x)
    for a,b in ALIAS.items(): setattr(r,a,getattr(r,b))
    for ph in phases: ph(r)
def compute(sl,mol,og,sp,bi,w1,wi,wu,phases=PHASES):
    V=pl.BlockSpec(memory_space=pltpu.VMEM)
    return pl.pallas_call(functools.partial(kernel,phases),
      out_shape=[jax.ShapeDtypeStruct(s,d) for _,s,d in OUTS],
      in_specs=[pl.BlockSpec(memory_space=pltpu.SMEM)]+[V]*7,out_specs=[V]*len(OUTS),
      scratch_shapes=[pltpu.VMEM(s,d) for _,s,d in SCR],
      compiler_params=pltpu.CompilerParams(vmem_limit_bytes=67043328))(sl,mol,og,sp,bi,w1,wi,wu)

F32=jnp.float32; BF=jnp.bfloat16
MESH=pl.DeviceIdType.MESH
def place():
    dp=lax.axis_index("dp"); fs=lax.axis_index("fsdp")
    return dp//2, dp%2, fs//2, fs%2
def dev(y,x,z,c): return (y*2+x, z*2+c)
class Here:
    def __init__(s):
        s.y,s.x,s.z,s.c=place()
        y,x,z,c=s.y,s.x,s.z,s.c
        s.partner=dev(y,x,z,1-c)
        py=jnp.where(c==0,y,1-y); px=jnp.where(c==0,1-x,x)
        qy=jnp.where(c==0,1-y,y); qx=jnp.where(c==0,x,1-x)
        s.p=dev(py,px,z,c); s.q=dev(qy,qx,z,c)
        s.zp=[dev(y,x,lax.rem(z+d,4),c) for d in (1,2,3)]
        s.line=y*2+x; s.pline=py*2+px; s.qline=qy*2+qx; s.pqline=(1-y)*2+(1-x)
        s.chip=s.line*4+s.z
        s.peers=[s.partner,s.p,s.q]+s.zp
def barrier(h):
    bar=pltpu.get_barrier_semaphore()
    for p in h.peers: pl.semaphore_signal(bar,inc=1,device_id=p,device_id_type=MESH)
    pl.semaphore_wait(bar,len(h.peers))
def remote(src,dst,ss,rs,dev): return pltpu.make_async_remote_copy(src_ref=src,dst_ref=dst,send_sem=ss,recv_sem=rs,device_id=dev,device_id_type=MESH)
def al(i,n): return pl.multiple_of(i*n,n)
NAG=19
class Gather:
    def __init__(s,h,W,rb,ch,off,width,ss,rs):
        s.h=h; s.W=W; s.rb=rb; s.ch=ch; s.off=off; s.width=width; s.ss=ss; s.rs=rs; s.started=[]
    def cols(s,c): return pl.ds(pl.multiple_of(c*s.ch+s.off,128),s.width)
    def blk(s,k,n=1): return s.W.at[pl.ds(al(k,s.rb),n*s.rb),s.cols(s.h.c)]
    def mk(s,i,k,n,dev,krecv):
        src=s.blk(k,n)
        return remote(src,src,s.ss.at[i],s.rs.at[i],dev)
    def go(s,i,k,n,dev):
        cp=s.mk(i,k,n,dev,None); cp.start(); s.started.append(cp)
    def arrived(s,i,k,n=1):
        b=s.blk(k,n); remote(b,b,s.ss.at[i],s.rs.at[i],s.h.partner).wait_recv()
    def zchip(s,d): return s.h.line*4+lax.rem(s.h.z+d,4)
    def own(s):
        h=s.h
        for d in (1,2,3): s.go(d-1,h.chip,1,h.zp[d-1])
        s.go(7,h.chip,1,h.q); s.go(3,h.chip,1,h.p)
    def zrelay(s,d):
        h=s.h; k=s.h.line*4+lax.rem(h.z+4-d,4)
        s.arrived(d-1,k); s.go(7+d,k,1,h.q); s.go(3+d,k,1,h.p)
    def zdone(s): s.go(15,s.h.line*4,4,s.h.partner)
    def prelay(s,d):
        h=s.h; k=h.pline*4+lax.rem(h.z+4-d,4)
        s.arrived(3+d,k); s.go(11+d,k,1,h.q)
    def pdone(s): s.go(16,s.h.pline*4,4,s.h.partner)
    def qwait(s):
        h=s.h
        for d in range(4): s.arrived(7+d,h.qline*4+lax.rem(h.z+4-d,4))
        s.go(17,h.qline*4,4,h.partner)
    def pqwait(s):
        h=s.h
        for d in range(4): s.arrived(11+d,h.pqline*4+lax.rem(h.z+4-d,4))
        s.go(18,h.pqline*4,4,h.partner)
    def fin(s):
        h=s.h
        for i,l in ((15,h.line),(16,h.pline),(17,h.qline),(18,h.pqline)):
            b=s.W.at[pl.ds(al(l,4*s.rb),4*s.rb),s.cols(1-h.c)]
            remote(b,b,s.ss.at[i],s.rs.at[i],h.partner).wait_recv()
    def drain(s):
        for cp in s.started: cp.wait_send()
def assemble(h,W,rb,ch,mine,theirs):
    a=mine.astype(F32); b=theirs.astype(F32)
    first=jnp.where(h.c==0,a,b); second=jnp.where(h.c==0,b,a)
    W[pl.ds(al(h.chip,rb),rb),pl.ds(pl.multiple_of(h.c*ch,128),ch)]=jnp.concatenate([first,second],axis=0).astype(BF)
NRS=8
class Scatter:
    def __init__(s,h,G,own,oth,rb,off,width,Rb,B,C,D,E,O,ss,rs):
        s.__dict__.update(locals()); s.ch=O.shape[1]//2
        s.w=pl.ds(off,width); s.started=[]
    def go(s,cp): cp.start(); s.started.append(cp)
    def pair(s):
        s.go(remote(s.G.at[s.oth,:,s.w],s.Rb,s.ss.at[0],s.rs.at[0],s.h.partner))
    def pair_wait(s):
        remote(s.Rb,s.Rb,s.ss.at[0],s.rs.at[0],s.h.partner).wait_recv()
    def add(s,row,n,src):
        T=min(n,192)
        def body(i,_):
            rows=pl.ds(pl.multiple_of(row+i*T,16),T)
            s.G[s.own,rows,s.w]=s.G[s.own,rows,s.w]+src[pl.ds(al(i,T),T),:]
            return 0
        lax.fori_loop(0,n//T,body,0)
    def start4(s,i,away):
        h=s.h; y=jnp.where(away,1-h.y,h.y); x=jnp.where(away,1-h.x,h.x)
        return al(jnp.where(h.c==0,y*2+i,i*2+x),4*s.rb)
    def first(s,i):
        r=s.start4(i,True); n=4*s.rb
        s.add(r,n,s.Rb.at[pl.ds(r,n),:])
        s.go(remote(s.G.at[s.own,pl.ds(r,n),s.w],s.B.at[i],s.ss.at[1+i],s.rs.at[1+i],s.h.q))
    def stay(s,i):
        r=s.start4(i,False); n=4*s.rb
        s.add(r,n,s.Rb.at[pl.ds(r,n),:])
    def second(s):
        h=s.h; i=jnp.where(h.c==0,1-h.x,1-h.y); r=s.start4(i,False); n=4*s.rb
        for k in (0,1): remote(s.B.at[k],s.B.at[k],s.ss.at[1+k],s.rs.at[1+k],h.q).wait_recv()
        s.add(r,n,s.B.at[i])
        s.go(remote(s.G.at[s.own,pl.ds(r,n),s.w],s.C,s.ss.at[3],s.rs.at[3],h.p))
        i2=1-i; r2=s.start4(i2,False)
        s.add(r2,n,s.B.at[i2])
    def third(s):
        h=s.h; i=jnp.where(h.c==0,h.x,h.y); r=s.start4(i,False); n=4*s.rb
        remote(s.C,s.C,s.ss.at[3],s.rs.at[3],h.p).wait_recv()
        s.add(r,n,s.C)
        for d in (1,2,3):
            k=pl.ds(pl.multiple_of(r+lax.rem(h.z+d,4)*s.rb,16),s.rb)
            s.go(remote(s.G.at[s.own,k,s.w],s.D.at[d-1],s.ss.at[3+d],s.rs.at[3+d],h.zp[d-1]))
    def fourth(s):
        h=s.h; i=jnp.where(h.c==0,h.x,h.y); r=s.start4(i,False)
        k=pl.ds(pl.multiple_of(r+h.z*s.rb,16),s.rb)
        t=s.G[s.own,k,s.w].astype(F32)
        for d in (1,2,3):
            remote(s.D.at[d-1],s.D.at[d-1],s.ss.at[3+d],s.rs.at[3+d],h.partner).wait_recv()
            t=t+s.D[d-1].astype(F32)
        s.E[...]=t
        hb=s.rb//2
        oc=pl.ds(pl.multiple_of(h.c*s.ch+s.off,128),s.width)
        src=s.E.at[pl.ds(al(1-h.c,hb),hb),:]
        s.go(remote(src,s.O.at[:,oc],s.ss.at[7],s.rs.at[7],h.partner))
        s.O[:,oc]=s.E[pl.ds(al(h.c,hb),hb),:]
    def fin(s):
        h=s.h; oc=pl.ds(pl.multiple_of((1-h.c)*s.ch+s.off,128),s.width)
        remote(s.O.at[:,oc],s.O.at[:,oc],s.ss.at[7],s.rs.at[7],h.partner).wait_recv()
        for cp in s.started: cp.wait_send()

def owner_rows(width, base):
    n=lax.broadcasted_iota(jnp.int32,(width,768),1)+base
    i=lax.broadcasted_iota(jnp.int32,(width,768),0)
    return lax.rem(n,width)==i
def owner_of(width, base, order):
    d=lax.broadcasted_iota(jnp.int32,(32,768),0)
    if order: d=lax.rem(d,16)*2+d//16
    n=lax.broadcasted_iota(jnp.int32,(32,768),1)+base
    return jnp.logical_and(n>=d*width,n<d*width+width).astype(F32)
class SmallGather:
    def __init__(s,h,S,ss,rs): s.h=h; s.S=S; s.ss=ss; s.rs=rs; s.started=[]
    def go(s,i,k,n,dev):
        b=s.S.at[pl.ds(k,n)]; cp=remote(b,b,s.ss.at[i],s.rs.at[i],dev); cp.start(); s.started.append(cp)
    def wait(s,i,k,n):
        b=s.S.at[pl.ds(k,n)]; remote(b,b,s.ss.at[i],s.rs.at[i],s.h.partner).wait_recv()
    def one(s,mine):
        h=s.h; s.S[pl.ds(h.chip*2+h.c,1)]=mine[None]; s.go(0,h.chip*2+h.c,1,h.partner)
    def two(s):
        h=s.h; s.wait(0,h.chip*2+1-h.c,1)
        for d in (1,2,3): s.go(d,h.chip*2,2,h.zp[d-1])
    def three(s):
        h=s.h
        for d in (1,2,3): s.wait(d,(h.line*4+lax.rem(h.z+4-d,4))*2,2)
        s.go(4,h.line*8,8,h.p); s.go(5,h.line*8,8,h.q)
    def four(s):
        h=s.h; s.wait(4,h.pline*8,8); s.go(6,h.pline*8,8,h.q)
    def five(s):
        h=s.h; s.wait(5,h.qline*8,8); s.wait(6,h.pqline*8,8)
        for cp in s.started: cp.wait_send()
def unpack(S,sp,bi):
    t=jnp.concatenate([S[:,k,:] for k in range(3)],axis=1).astype(BF)
    u=tn(t,owner_of(24,0,False).astype(BF))
    keep=owner_rows(24,0)
    for j in range(8):
        sp[j:j+1,:]=jnp.sum(jnp.where(keep,u[24*j:24*j+24],0.0),axis=0,keepdims=True)
    for k in range(4):
        u=tn(t,owner_of(96,768*k,False).astype(BF))
        bi[0:1,768*k:768*k+768]=jnp.sum(jnp.where(owner_rows(96,768*k),u[192:288],0.0),axis=0,keepdims=True)
def pack(sg,sgi,M):
    keep=owner_rows(24,0)
    z=jnp.zeros((96,768),F32)
    y=jnp.concatenate([jnp.where(keep,sg[j:j+1,:],0.0) for j in range(8)]+[z,z],axis=0)
    dot=lambda a,b: lax.dot_general(a,b,(((1,),(1,)),((),())),precision=lax.Precision.HIGHEST,preferred_element_type=F32)
    m=dot(owner_of(24,0,True),y)
    for k in range(4):
        y=jnp.concatenate([z,z,jnp.where(owner_rows(96,768*k),sgi[0:1,768*k:768*k+768],0.0),z],axis=0)
        m=m+dot(owner_of(96,768*k,True),y)
    for r in range(3):
        for c in range(2): M[c,:,r,:]=m[16*c:16*c+16,128*r:128*r+128]
class SmallScatter:
    def __init__(s,h,M,Rb,B,C,D,O,ss,rs): s.__dict__.update(locals()); s.started=[]
    def go(s,i,src,dst,dev):
        cp=remote(src,dst,s.ss.at[i],s.rs.at[i],dev); cp.start(); s.started.append(cp)
    def wait(s,i,dst): remote(dst,dst,s.ss.at[i],s.rs.at[i],s.h.partner).wait_recv()
    def start4(s,i,away):
        h=s.h; y=jnp.where(away,1-h.y,h.y); x=jnp.where(away,1-h.x,h.x)
        return jnp.where(h.c==0,y*2+i,i*2+x)*4
    def one(s): s.go(0,s.M.at[1-s.h.c],s.Rb,s.h.partner)
    def two(s):
        h=s.h; s.wait(0,s.Rb)
        s.M[h.c]=s.M[h.c]+s.Rb[...]
        for i in (0,1): s.go(1+i,s.M.at[h.c,pl.ds(s.start4(i,True),4)],s.B.at[i],h.q)
    def three(s):
        h=s.h
        for i in (0,1):
            s.wait(1+i,s.B.at[i]); k=pl.ds(s.start4(i,False),4)
            s.M[h.c,k]=s.M[h.c,k]+s.B[i]
        s.go(3,s.M.at[h.c,pl.ds(s.start4(jnp.where(h.c==0,1-h.x,1-h.y),False),4)],s.C,h.p)
    def four(s):
        h=s.h; s.wait(3,s.C); r=s.start4(jnp.where(h.c==0,h.x,h.y),False)
        s.M[h.c,pl.ds(r,4)]=s.M[h.c,pl.ds(r,4)]+s.C[...]
        for d in (1,2,3): s.go(3+d,s.M.at[h.c,pl.ds(r+lax.rem(h.z+d,4),1)],s.D.at[pl.ds(d-1,1)],h.zp[d-1])
    def five(s):
        h=s.h; r=s.start4(jnp.where(h.c==0,h.x,h.y),False)
        t=s.M[h.c,pl.ds(r+h.z,1)][0]
        for d in (1,2,3):
            s.wait(3+d,s.D.at[pl.ds(d-1,1)]); t=t+s.D[d-1]
        s.O[...]=t
        for cp in s.started: cp.wait_send()
def histogram(ids,CN):
    i=lax.broadcasted_iota(jnp.int32,(128,1),0)
    def body(k,_):
        v=ids[pl.ds(k,1),:]
        hi=jnp.where(i==lax.shift_right_logical(v,7),1.0,0.0).astype(BF)
        lo=jnp.where(i==jnp.bitwise_and(v,127),1.0,0.0).astype(BF)
        c=nt(hi,lo)
        CN[0,pl.ds(k,64,stride=8),:]=c[0:64]
        CN[1,pl.ds(k,64,stride=8),:]=c[64:128]
        return 0
    lax.fori_loop(0,8,body,0)
class CountScatter(Scatter):
    def fourth(s):
        h=s.h; i=jnp.where(h.c==0,h.x,h.y); r=s.start4(i,False)
        t=s.G[s.own,pl.ds(pl.multiple_of(r+h.z*s.rb,8),s.rb),:]
        for d in (1,2,3):
            remote(s.D.at[d-1],s.D.at[d-1],s.ss.at[3+d],s.rs.at[3+d],h.partner).wait_recv()
            t=t+s.D[d-1]
        for k in range(4):
            s.O[:,pl.ds(pl.multiple_of((h.c*64+h.chip*4+k)*128,128),128)]=t[8*k:8*k+8].astype(jnp.int32)
    def fin(s):
        for cp in s.started: cp.wait_send()
class CountGather(Gather):
    def blk(s,k,n=1): return s.W.at[:,pl.ds(pl.multiple_of((s.h.c*64+k*4)*128,512),n*512)]
    def fin(s):
        h=s.h
        for i,l in ((15,h.line),(16,h.pline),(17,h.qline),(18,h.pqline)):
            b=s.W.at[:,pl.ds(pl.multiple_of(((1-h.c)*64+l*16)*128,2048),2048)]
            remote(b,b,s.ss.at[i],s.rs.at[i],h.partner).wait_recv()
VM=pl.BlockSpec(memory_space=pltpu.VMEM)
SUB1=2; SUBU=1
AGCH=[("w1",k) for k in range(SUB1)]+[("wi",k) for k in range(SUB1)]+[("wu",k) for k in range(SUBU)]
def gather_kernel(wq,wk,wv,wo,wi_s,wu_s,spk,ids,w1,wi,wu,sp,bi,cnt,P4,Pi,Pu,S,CN,Rb,B,C,D,s1,r1,ag_s,ag_r,sm_s,sm_r,cs_s,cs_r,cg_s,cg_r):
    h=Here(); c=h.c
    barrier(h)
    half=lambda n,k: pl.ds(pl.multiple_of(k*n,128),n)
    st=[remote(a,P4.at[k],s1.at[k],r1.at[k],h.partner) for k,a in enumerate((wq,wk,wv,wo))]
    st+=[remote(wi_s.at[:,half(1536,1-c)],Pi,s1.at[4],r1.at[4],h.partner),remote(wu_s.at[:,half(384,1-c)],Pu,s1.at[5],r1.at[5],h.partner)]
    for t in st: t.start()
    sg=SmallGather(h,S,sm_s,sm_r); sg.one(spk[...])
    G=[]
    for i,(n,k) in enumerate(AGCH):
        W,rb,ch,sub={"w1":(w1,48,1536,SUB1),"wi":(wi,48,1536,SUB1),"wu":(wu,192,384,SUBU)}[n]
        G.append(Gather(h,W,rb,ch,k*(ch//sub),ch//sub,ag_s.at[i],ag_r.at[i]))
    for t in st[:4]: t.wait_recv()
    cat=lambda a,b,e,f: jnp.where(c==0,jnp.concatenate([a,b],1).astype(F32),jnp.concatenate([e,f],1).astype(F32))
    assemble(h,w1,48,1536,cat(wq[...],wk[...],wv[...],wo[...]),cat(P4[0],P4[1],P4[2],P4[3]))
    st[4].wait_recv(); assemble(h,wi,48,1536,wi_s[:,half(1536,c)],Pi[...])
    st[5].wait_recv(); assemble(h,wu,192,384,wu_s[:,half(384,c)],Pu[...])
    for g in G: g.own()
    sg.two()
    histogram(ids,CN)
    cs=CountScatter(h,CN,c,1-c,32,0,128,Rb,B,C,D,None,cnt,cs_s,cs_r)
    cg=CountGather(h,cnt,None,None,0,None,cg_s,cg_r)
    cs.pair(); sg.three(); sg.four(); cs.pair_wait(); cs.first(0); cs.first(1); cs.stay(0); cs.stay(1)
    sg.five(); unpack(S,sp,bi)
    cs.second(); cs.third(); cs.fourth(); cg.own()
    for g in G+[cg]:
        for d in (1,2,3): g.zrelay(d)
        g.zdone()
        g.prelay(0)
        for d in (1,2,3): g.prelay(d)
        g.pdone()
    for g in G+[cg]: g.qwait(); g.pqwait()
    for g in G+[cg]: g.fin()
    for g in G+[cg]: g.drain()
    cs.fin()
    for t in st: t.wait_send()
def sems(*n): return [pltpu.SemaphoreType.DMA(n),pltpu.SemaphoreType.DMA(n)]
def gather_call(wq,wk,wv,wo,wi,wu,spk,ids):
    S=lambda s,d: jax.ShapeDtypeStruct(s,d)
    return pl.pallas_call(gather_kernel,
        out_shape=[S((768,3072),BF),S((768,3072),BF),S((3072,768),BF),S((8,768),F32),S((1,3072),F32),S((8,16384),jnp.int32)],
        in_specs=[VM]*8,out_specs=[VM]*6,
        scratch_shapes=[pltpu.VMEM((4,24,768),BF),pltpu.VMEM((24,1536),BF),pltpu.VMEM((96,384),BF),pltpu.VMEM((32,8,128),F32),
            pltpu.VMEM((2,512,128),F32),pltpu.VMEM((512,128),F32),pltpu.VMEM((2,128,128),F32),pltpu.VMEM((128,128),F32),pltpu.VMEM((3,32,128),F32)]
            +sems(6)+sems(len(AGCH),NAG)+sems(7)+sems(NRS)+sems(NAG),
        compiler_params=pltpu.CompilerParams(collective_id=0,has_side_effects=True,vmem_limit_bytes=67043328))(wq,wk,wv,wo,wi,wu,spk,ids)
def scatter_kernel(g1,gi,gu,sg,sgi,o1,oi,ou,os,*scr):
    h=Here(); c=h.c
    barrier(h)
    n=5; bufs=[scr[n*k:n*k+n] for k in range(3)]; M,mRb,mB,mC,mD=scr[15:20]; ss,rs,ms,mr=scr[20:]
    X=[Scatter(h,G,c,1-c,rb,0,w,*b,O,ss.at[k],rs.at[k]) for k,(G,rb,w,O,b) in enumerate(((gu,192,384,ou,bufs[0]),(gi,48,1536,oi,bufs[1]),(g1,48,1536,o1,bufs[2])))]
    pack(sg,sgi,M)
    sm=SmallScatter(h,M,mRb,mB,mC,mD,os,ms,mr); sm.one()
    for x in X: x.pair()
    sm.two()
    for x in X:
        x.pair_wait()
        for i in (0,1): x.first(i)
        for i in (0,1): x.stay(i)
    sm.three(); sm.four()
    for x in X: x.second()
    for x in X: x.third()
    sm.five()
    for x in X: x.fourth()
    for x in X: x.fin()
def scatter_call(g1,gi,gu,sg,sgi):
    S=lambda s,d: jax.ShapeDtypeStruct(s,d)
    scr=[]
    for rb,w in ((192,384),(48,1536),(48,1536)):
        scr+=[pltpu.VMEM((16*rb,w),BF),pltpu.VMEM((2,4*rb,w),BF),pltpu.VMEM((4*rb,w),BF),pltpu.VMEM((3,rb,w),BF),pltpu.VMEM((rb,w),F32)]
    scr+=[pltpu.VMEM((2,16,8,128),F32),pltpu.VMEM((16,8,128),F32),pltpu.VMEM((2,4,8,128),F32),pltpu.VMEM((4,8,128),F32),pltpu.VMEM((3,8,128),F32)]
    scr+=sems(3,NRS)+sems(7)
    return pl.pallas_call(scatter_kernel,
        out_shape=[S((24,3072),F32),S((24,3072),F32),S((96,768),F32),S((8,128),F32)],
        in_specs=[VM]*5,out_specs=[VM]*4,scratch_shapes=scr,
        compiler_params=pltpu.CompilerParams(collective_id=1,has_side_effects=True,vmem_limit_bytes=67043328))(g1,gi,gu,sg,sgi)
def local(mol,lens,ids,og,*par):
    (l1g,l1b,wq,bq,wk,wv,bv,wo,bo,l2g,l2b,wi,bi,wu,bu)=par
    spk=jnp.concatenate([l1g,l1b,bq,bv,bo,l2g,l2b,bu,bi]).astype(F32)
    spk=jnp.pad(spk,(0,1024-spk.shape[0])).reshape(8,128)
    w1,wif,wuf,sp,bif,cnt=gather_call(wq,wk,wv,wo,wi,wu,spk,ids)
    out,ing,g1,gi,gu,sg,sgi=compute(lens,mol[0],og[0],sp,bif,w1,wif,wuf)
    o1,oi,ou,os=scatter_call(g1,gi,gu,sg,sgi)
    sm=os.reshape(1024)
    s=[sm[24*k:24*k+24] for k in range(8)]
    w=[o1[:,768*k:768*k+768] for k in range(4)]
    return (out[None],ing[None],s[0],s[1],w[0],s[2],w[1],w[2],s[3],w[3],s[4],s[5],s[6],oi,sm[192:288],ou,s[7],cnt)
BUCKETS=16384
def hist_call(ids):
    return pl.pallas_call(lambda i,o: histogram(i,o),out_shape=jax.ShapeDtypeStruct((2,512,128),F32),in_specs=[VM],out_specs=VM)(ids)
def local_xla(mol,lens,ids,og,*par):
    a=("dp","fsdp")
    full=[lax.all_gather(p,a,axis=0,tiled=True) for p in par]
    (l1g,l1b,wq,bq,wk,wv,bv,wo,bo,l2g,l2b,wi,bi,wu,bu)=full
    sp=jnp.stack([l1g,l1b,bq,bv,bo,l2g,l2b,bu]).astype(F32)
    out,ing,g1,gi,gu,sg,sgi=compute(lens,mol[0],og[0],sp,bi.astype(F32)[None],jnp.concatenate([wq,wk,wv,wo],axis=1),wi,wu)
    rs=lambda g: lax.psum_scatter(g.astype(F32),a,scatter_dimension=0,tiled=True)
    s=[rs(sg[k]) for k in range(8)]
    w=[rs(g1[k//2][:,768*(k%2):768*(k%2)+768]) for k in range(4)]
    gi=rs(jnp.concatenate([gi[0],gi[1]],axis=1)); gu=rs(jnp.concatenate([gu[0],gu[1]],axis=1))
    cnt=lax.psum(hist_call(ids),a).reshape(128,8,128).transpose(1,0,2).reshape(8,BUCKETS).astype(jnp.int32)
    return (out[None],ing[None],s[0],s[1],w[0],s[2],w[1],w[2],s[3],w[3],s[4],s[5],s[6],gi,rs(sgi[0]),gu,s[7],cnt)
def solution(mesh):
    a=("dp","fsdp"); r=P(a); r2=P(a,None); r3=P(a,None,None)
    in_specs=(r3,r,P(None,a),r3,r,r,r2,r,r2,r2,r,r2,r,r,r,r2,r,r2,r)
    out_specs=(r3,r3,r,r,r2,r,r2,r2,r,r2,r,r,r,r2,r,r2,r,P())
    body=local if dict(mesh.shape)=={"dp":4,"fsdp":8} else local_xla
    return jax.shard_map(body,mesh=mesh,in_specs=in_specs,out_specs=out_specs,check_vma=False)
```

```python
import functools

import jax
import jax.numpy as jnp
from jax import lax
from jax.experimental import pallas as pl
from jax.experimental.pallas import tpu as pltpu
from jax.sharding import PartitionSpec as P

F32 = jnp.float32
BF = jnp.bfloat16
I32 = jnp.int32
MESH = pl.DeviceIdType.MESH
VM = pl.BlockSpec(memory_space=pltpu.VMEM)
EPS = 1e-5
RSQRT2 = 0.7071067811865476
RSQRT2PI = 0.3989422804014327
VMEM_BYTES = 67043328
T, D, FF, PAIRS, BUCKETS = 512, 768, 3072, 6, 16384
ROWT = 128
CT = 256


def mm(a, b):
    return lax.dot_general(a, b, (((1,), (0,)), ((), ())), preferred_element_type=F32)


def nt(a, b):
    return lax.dot_general(a, b, (((1,), (1,)), ((), ())), preferred_element_type=F32)


def tn(a, b):
    return lax.dot_general(a, b, (((0,), (0,)), ((), ())), preferred_element_type=F32)


def at(i, n):
    return pl.multiple_of(i * n, n)


def ds(i, n):
    return pl.ds(at(i, n), n)


def loop(n, body):
    def step(i, carry):
        body(i)
        return carry

    lax.fori_loop(0, n, step, 0)


def norm_rows(v):
    cen = v - jnp.mean(v, axis=-1, keepdims=True)
    r = lax.rsqrt(jnp.mean(cen * cen, axis=-1, keepdims=True) + EPS)
    return cen * r, r


def ln1(r):
    g, b = r.sp[0:1, :], r.sp[1:2, :]

    def body(i):
        n, _ = norm_rows(r.mol[ds(i, ROWT), :].astype(F32))
        r.nrm[ds(i, ROWT), :] = (n * g + b).astype(BF)

    loop(T // ROWT, body)


def qkv(r):
    def body(j):
        n = r.nrm[...]
        c = ds(j, CT)
        w = lambda m: r.w1[m, :, :, c].reshape(D, CT)
        q = mm(n, w(0)) + r.sp[2:3, c]
        r.q[:, c] = (q.astype(BF).astype(F32) * 0.125).astype(BF)
        r.k[:, c] = mm(n, w(1)).astype(BF)
        r.v[:, c] = (mm(n, w(2)) + r.sp[3:4, c]).astype(BF)

    loop(D // CT, body)


def low_half():
    return lax.broadcasted_iota(I32, (1, 128), 1) < 64


def attn_fwd(r, first, last):
    def body(j):
        lo = low_half()
        kpos = lax.broadcasted_iota(I32, (T, 128), 0)
        bias = jnp.where(kpos < r.sl[0], 0.0, -1e30 / 64).astype(BF)
        c = ds(j + first, 128)
        q2, k2, v2 = r.q[:, c], r.k[:, c], r.v[:, c]
        one = jnp.ones((), BF)
        outs = []
        for h in (0, 1):
            half = lo if h == 0 else jnp.logical_not(lo)
            s = nt(jnp.where(half, q2, one), jnp.where(half, k2, bias))
            p = jnp.exp(s - jnp.max(s, axis=-1, keepdims=True)).astype(BF)
            r.p[2 * (j + first) + h] = p
            outs.append(mm(p, jnp.where(half, v2, one)))
        rl = 1.0 / pltpu.roll(jnp.where(lo, outs[1], outs[0]), 64, 1)
        r.rl[:, c] = rl
        r.ctx[:, c] = (jnp.where(lo, outs[0], outs[1]) * rl).astype(BF)

    loop(last - first, body)


def outproj(r):
    def body(j):
        c = ds(j, CT)
        r.mid[:, c] = r.mol[:, c].astype(F32) + (
            mm(r.ctx[...], r.w1[3, :, :, c].reshape(D, CT)) + r.sp[4:5, c]
        )

    loop(D // CT, body)


def ln2(r):
    g, b = r.sp[5:6, :], r.sp[6:7, :]

    def body(i):
        n, _ = norm_rows(r.mid[ds(i, ROWT), :])
        v = n * g + b
        r.n2T[:, ds(i, ROWT)] = v.T.astype(BF)
        r.n2[ds(i, ROWT), :] = v.astype(BF)

    loop(T // ROWT, body)


def inner(r, s):
    def body(i):
        j = i + 2 * (i // 2) + 2 * s
        c = ds(j, 384)
        w = r.wi[j // 2, :, :, ds(lax.rem(j, 2), 384)].reshape(D, 384)
        u = mm(r.n2[...], w) + r.bi[0:1, c]
        ph = 0.5 + 0.5 * lax.erf(u * RSQRT2)
        hid = (u * ph).astype(BF)
        r.hid[:, c] = hid
        r.gp[:, c] = (ph + u * (RSQRT2PI * jnp.exp(-0.5 * u * u))).astype(BF)
        t = tn(hid, r.og[...]).astype(BF).reshape(2, 4, 48, D)
        for k in range(4):
            r.G[r.slot(0, k // 2, k % 2), pl.ds(2 * j, 2)] = t[:, k]

    loop(4, body)


def grad_top_sum(r):
    def body(i, a):
        return a + jnp.sum(r.og[ds(i, ROWT), :].astype(F32), axis=0, keepdims=True)

    r.sg[7:8, :] = lax.fori_loop(0, T // ROWT, body, jnp.zeros((1, D), F32))


def outp(r):
    def body(j):
        c = ds(j, CT)
        w = r.wu[:, :, :, c].reshape(FF, CT)
        low = pl.ds(pl.multiple_of(D + j * CT, CT), CT)
        mid = r.gp[:, c].astype(F32) + r.gp[:, low].astype(F32)
        r.out[:, c] = (mid + (mm(r.hid[...], w) + r.sp[7:8, c])).astype(BF)

    loop(D // CT, body)


def ginner(r, first, n):
    def body(k):
        i = first + 2 * k
        w = r.wu[ds(i, 4)].reshape(D, D)
        for t in range(3):
            c = pl.ds(pl.multiple_of(i * D + CT * t, CT), CT)
            gi = nt(r.og[...], w[CT * t : CT * t + CT]) * r.gp[:, c].astype(F32)
            r.sgi[0:1, c] = jnp.sum(gi, axis=0, keepdims=True)
            gib = gi.astype(BF)
            r.gp[:, c] = gib
            r.G[r.slot(1, i // 2, lax.rem(i, 2)), :, :, CT * t : CT * t + CT] = (
                mm(r.n2T[...], gib).astype(BF).reshape(16, 48, CT)
            )

    loop(n, body)


def gn2(r):
    def body(j):
        e = None
        for i in range(4):
            w = r.wi[i, pl.ds(8 * j, 8)].reshape(384, D)
            t = nt(r.gp[:, D * i : D * i + D], w)
            e = t if e is None else e + t
        r.e[:, ds(j, 384)] = e

    loop(2, body)


def ln_bwd(r, src, gain_row, first):
    gain = r.sp[gain_row : gain_row + 1, :]

    def body(i, a):
        rows = ds(i, ROWT)
        v = src[rows, :].astype(F32)
        n, rs = norm_rows(v)
        e = r.e[rows, :]
        eg = e * gain
        m1 = jnp.mean(eg, axis=-1, keepdims=True)
        m2 = jnp.mean(eg * n, axis=-1, keepdims=True)
        gv = rs * (eg - m1 - n * m2)
        a0 = a[0] + jnp.sum(e * n, axis=0, keepdims=True)
        a1 = a[1] + jnp.sum(e, axis=0, keepdims=True)
        if first:
            r.ing[rows, :] = (r.mid[rows, :] + gv).astype(BF)
            return (a0, a1)
        gm = r.og[rows, :].astype(F32) + gv
        hi = v.astype(BF)
        r.gp[rows, 0:D] = hi
        r.gp[rows, D : 2 * D] = (v - hi.astype(F32)).astype(BF)
        r.mid[rows, :] = gm
        r.n2[rows, :] = gm.astype(BF)
        return (a0, a1, a[2] + jnp.sum(gm, axis=0, keepdims=True))

    z = jnp.zeros((1, D), F32)
    return lax.fori_loop(0, T // ROWT, body, (z, z) if first else (z, z, z))


def ln2b(r):
    a = ln_bwd(r, r.mid, 5, False)
    r.sg[5:6, :] = a[0]
    r.sg[6:7, :] = a[1]
    r.sg[4:5, :] = a[2]


def gctx(r):
    def body(j):
        c = ds(j, 384)
        k = pl.ds(8 * j, 8)
        g = tn(r.ctx[:, c], r.n2[...]).astype(BF).reshape(8, 48, D)
        for s in range(2):
            r.G[r.slot(2, 1, s), k, :, 384:768] = g[:, :, 384 * s : 384 * s + 384]
        r.gc[:, c] = nt(r.n2[...], r.w1[3, k].reshape(384, D)).astype(BF)

    loop(2, body)


def attn_bwd(r, first, last):
    def body(j):
        lo = low_half()
        c = ds(j + first, 128)
        q2, k2, v2 = r.q[:, c], r.k[:, c], r.v[:, c]
        gp = r.gc[:, c].astype(F32) * r.rl[:, c]
        dd = r.ctx[:, c].astype(F32) * gp
        gpb = gp.astype(BF)
        zero = jnp.zeros((), BF)
        gT = gp.T.astype(BF)
        qT = q2.astype(F32).T.astype(BF)
        dq, dkT, dvT = [], [], []
        for h in (0, 1):
            half = lo if h == 0 else jnp.logical_not(lo)
            dsum = jnp.sum(jnp.where(half, dd, 0.0), axis=-1, keepdims=True)
            dp = nt(jnp.where(half, gpb, zero), v2)
            p = r.p[2 * (j + first) + h]
            dsl = (p.astype(F32) * (dp - dsum)).astype(BF)
            dq.append(mm(dsl, k2))
            dvT.append(mm(gT[64 * h : 64 * h + 64], p))
            dkT.append(mm(qT[64 * h : 64 * h + 64], dsl))
        gq = jnp.where(lo, dq[0], dq[1]) * 0.125
        gv = jnp.concatenate(dvT, axis=0).T
        gk = jnp.concatenate(dkT, axis=0).T
        r.sg[2:3, c] = jnp.sum(gq, axis=0, keepdims=True)
        r.sg[3:4, c] = jnp.sum(gv, axis=0, keepdims=True)
        r.gc[:, c] = gq.astype(BF)
        r.k[:, c] = gk.astype(BF)
        r.v[:, c] = gv.astype(BF)

    loop(last - first, body)


def gw1(r, s):
    def body(j):
        n = r.nrm[:, ds(j, 384)]
        k = pl.ds(8 * j, 8)
        for h, t, g in ((0, 0, r.gc), (0, 384, r.k), (1, 0, r.v)):
            d = tn(n, g[:, 384 * s : 384 * s + 384]).astype(BF)
            r.G[r.slot(2, h, s), k, :, t : t + 384] = d.reshape(8, 48, 384)

    loop(2, body)


def gn1(r):
    def body(j):
        k = pl.ds(8 * j, 8)
        e = None
        for m, g in enumerate((r.gc, r.k, r.v)):
            t = nt(g[...], r.w1[m, k].reshape(384, D))
            e = t if e is None else e + t
        r.e[:, ds(j, 384)] = e

    loop(2, body)


def ln1b(r):
    a = ln_bwd(r, r.mol, 0, True)
    r.sg[0:1, :] = a[0]
    r.sg[1:2, :] = a[1]


ACTS = [
    ("nrm", (T, D), BF), ("k", (T, D), BF), ("v", (T, D), BF), ("p", (12, T, T), BF),
    ("rl", (T, D), F32), ("ctx", (T, D), BF), ("mid", (T, D), F32), ("n2T", (D, T), BF),
    ("hid", (T, FF), BF), ("gp", (T, FF), BF), ("e", (T, D), F32),
]


class Refs:
    pass


def histogram(ids, CN):
    i = lax.broadcasted_iota(I32, (128, 1), 0)

    def body(k):
        v = ids[pl.ds(k, 1), :]
        hi = jnp.where(i == lax.shift_right_logical(v, 7), 1.0, 0.0).astype(BF)
        lo = jnp.where(i == jnp.bitwise_and(v, 127), 1.0, 0.0).astype(BF)
        c = nt(hi, lo)
        for half in range(2):
            for q in range(16):
                m = 64 * half + 4 * q
                CN[half, q, pl.ds(k, 4, stride=8), :] = c[m : m + 4]

    loop(8, body)


class Here:
    def __init__(s):
        dp, fs = lax.axis_index("dp"), lax.axis_index("fsdp")
        s.y, s.x, s.z, s.c = y, x, z, c = dp // 2, dp % 2, fs // 2, fs % 2
        dev = lambda y, x, z, c: (y * 2 + x, z * 2 + c)
        py, px = jnp.where(c == 0, y, 1 - y), jnp.where(c == 0, 1 - x, x)
        qy, qx = jnp.where(c == 0, 1 - y, y), jnp.where(c == 0, x, 1 - x)
        s.partner, s.p, s.q = dev(y, x, z, 1 - c), dev(py, px, z, c), dev(qy, qx, z, c)
        s.zp = [dev(y, x, lax.rem(z + d, 4), c) for d in (1, 2, 3)]
        s.line, s.pline, s.qline, s.pqline = y * 2 + x, py * 2 + px, qy * 2 + qx, (1 - y) * 2 + (1 - x)
        s.chip = s.line * 4 + s.z

    def before(s, line, d):
        return line * 4 + lax.rem(s.z + 4 - d, 4)

    def start4(s, i, away):
        y, x = jnp.where(away, 1 - s.y, s.y), jnp.where(away, 1 - s.x, s.x)
        return jnp.where(s.c == 0, y * 2 + i, i * 2 + x) * 4

    def keep(s):
        return jnp.where(s.c == 0, s.x, s.y)


class Copies:
    def __init__(s, h, sems):
        s.h, (s.ss, s.rs), s.started = h, sems, []

    def copy(s, i, src, dst, dev):
        return pltpu.make_async_remote_copy(
            src_ref=src, dst_ref=dst, send_sem=s.ss.at[i], recv_sem=s.rs.at[i], device_id=dev, device_id_type=MESH
        )

    def go(s, i, src, dst, dev):
        cp = s.copy(i, src, dst, dev)
        cp.start()
        s.started.append(cp)

    def wait(s, i, dst):
        s.copy(i, dst, dst, s.h.partner).wait_recv()

    def drain(s):
        for cp in s.started:
            cp.wait_send()


class Gather(Copies):
    def __init__(s, h, sems, blk):
        super().__init__(h, sems)
        s.blk = blk

    def send(s, i, k, n, dev):
        b = s.blk(s.h.c, k, n)
        s.go(i, b, b, dev)

    def come(s, i, k):
        s.wait(i, s.blk(s.h.c, k, 1))

    def own(s):
        h = s.h
        for d in (1, 2, 3):
            s.send(d - 1, h.chip, 1, h.zp[d - 1])
        s.send(7, h.chip, 1, h.q)
        s.send(3, h.chip, 1, h.p)

    def zrelay(s):
        h = s.h
        for d in (1, 2, 3):
            k = h.before(h.line, d)
            s.come(d - 1, k)
            s.send(7 + d, k, 1, h.q)
            s.send(3 + d, k, 1, h.p)
        s.send(15, h.line * 4, 4, h.partner)

    def prelay(s):
        h = s.h
        for d in range(4):
            k = h.before(h.pline, d)
            s.come(3 + d, k)
            s.send(11 + d, k, 1, h.q)
        s.send(16, h.pline * 4, 4, h.partner)

    def qwait(s):
        h = s.h
        for base, line, i in ((7, h.qline, 17), (11, h.pqline, 18)):
            for d in range(4):
                s.come(base + d, h.before(line, d))
            s.send(i, line * 4, 4, h.partner)

    def fin(s):
        h = s.h
        for i, line in ((15, h.line), (16, h.pline), (17, h.qline), (18, h.pqline)):
            s.wait(i, s.blk(1 - h.c, line * 4, 4))


class Sum(Copies):
    def __init__(s, h, sems, V, R, B, C, Dz):
        super().__init__(h, sems)
        s.V, s.R, s.B, s.C, s.Dz = V, R, B, C, Dz

    def pair(s, src):
        s.go(0, src, s.R, s.h.partner)

    def add(s, k, src):
        for i in range(4):
            s.V[k + i] = s.V[k + i] + src[i]

    def first(s):
        h = s.h
        s.wait(0, s.R)
        for i in (0, 1):
            k = h.start4(i, True)
            s.add(k, s.R.at[pl.ds(k, 4)])
            s.go(1 + i, s.V.at[pl.ds(k, 4)], s.B.at[i], h.q)
        for i in (0, 1):
            k = h.start4(i, False)
            s.add(k, s.R.at[pl.ds(k, 4)])

    def second(s):
        h = s.h
        for i in (0, 1):
            s.wait(1 + i, s.B.at[i])
        i = 1 - h.keep()
        k = h.start4(i, False)
        s.add(k, s.B.at[i])
        s.go(3, s.V.at[pl.ds(k, 4)], s.C, h.p)
        s.add(h.start4(1 - i, False), s.B.at[1 - i])

    def third(s):
        h = s.h
        s.wait(3, s.C)
        k = h.start4(h.keep(), False)
        s.add(k, s.C)
        for d in (1, 2, 3):
            s.go(3 + d, s.V.at[pl.ds(k + lax.rem(h.z + d, 4), 1)], s.Dz.at[pl.ds(d - 1, 1)], h.zp[d - 1])

    def total(s):
        h = s.h
        t = s.V[h.start4(h.keep(), False) + h.z].astype(F32)
        for d in (1, 2, 3):
            s.wait(3 + d, s.Dz.at[pl.ds(d - 1, 1)])
            t = t + s.Dz[d - 1].astype(F32)
        return t


def split_rows(s, E, O):
    c = s.h.c
    E[...] = s.total()
    s.go(7, E.at[ds(1 - c, 24)], O, s.h.partner)
    O[...] = E[ds(c, 24), :]


class SmallGather(Copies):
    def send(s, i, k, n, dev):
        b = s.S.at[pl.ds(k, n)]
        s.go(i, b, b, dev)

    def come(s, i, k, n):
        s.wait(i, s.S.at[pl.ds(k, n)])

    def one(s, S, shares):
        h = s.h
        s.S, me = S, h.chip * 2 + h.c
        S[me] = jnp.zeros((16, 128), F32)
        for j, p in enumerate(shares):
            n = p.shape[0]
            S[me, j : j + 1, 0:n] = p[...].astype(F32).reshape(1, n)
        s.send(0, me, 1, h.partner)

    def two(s):
        h = s.h
        s.come(0, h.chip * 2 + 1 - h.c, 1)
        for d in (1, 2, 3):
            s.send(d, h.chip * 2, 2, h.zp[d - 1])

    def three(s):
        h = s.h
        for d in (1, 2, 3):
            s.come(d, h.before(h.line, d) * 2, 2)
        s.send(4, h.line * 8, 8, h.p)
        s.send(5, h.line * 8, 8, h.q)

    def four(s):
        h = s.h
        s.come(4, h.pline * 8, 8)
        s.send(6, h.pline * 8, 8, h.q)

    def five(s):
        h = s.h
        s.come(5, h.qline * 8, 8)
        s.come(6, h.pqline * 8, 8)


def share_mask(rows, width, base):
    n = lax.broadcasted_iota(I32, (rows, D), 1) + base
    return lax.rem(n, width) == lax.broadcasted_iota(I32, (rows, D), 0)


def owner_mask(width, base, by_core):
    d = lax.broadcasted_iota(I32, (32, D), 0)
    if by_core:
        d = lax.rem(d, 16) * 2 + d // 16
    n = lax.broadcasted_iota(I32, (32, D), 1) + base
    return jnp.logical_and(n >= d * width, n < d * width + width).astype(F32)


def unpack(S, sp, bi):
    keep, own = share_mask(24, 24, 0), owner_mask(24, 0, False).astype(BF)
    for j in range(8):
        u = tn(S[:, j, :].astype(BF), own)
        sp[j : j + 1, :] = jnp.sum(jnp.where(keep, u[0:24], 0.0), axis=0, keepdims=True)
    t = S[:, 8, :].astype(BF)
    for k in range(4):
        u = tn(t, owner_mask(96, D * k, False).astype(BF))
        bi[0:1, D * k : D * k + D] = jnp.sum(
            jnp.where(share_mask(96, 96, D * k), u[0:96], 0.0), axis=0, keepdims=True
        )


def pack(sg, sgi, M):
    dot = lambda a, b: lax.dot_general(
        a, b, (((1,), (1,)), ((), ())), precision=lax.Precision.HIGHEST, preferred_element_type=F32
    )
    keep, own = share_mask(32, 24, 0), owner_mask(24, 0, True)
    rows = []
    for half in range(2):
        y = [jnp.where(keep, sg[4 * half + j : 4 * half + j + 1, :], 0.0) for j in range(4)]
        rows.append(dot(own, jnp.concatenate(y, axis=0)))
    t = None
    for k in range(4):
        y = jnp.where(share_mask(128, 96, D * k), sgi[0:1, D * k : D * k + D], 0.0)
        u = dot(owner_mask(96, D * k, True), y)
        t = u if t is None else t + u
    rows.append(t)
    for i, m in enumerate(rows):
        for c in range(2):
            M[c, :, i, :] = m[16 * c : 16 * c + 16]


N_GATHER, N_SUM = 19, 8


def layer_kernel(sl, mol, og, ids, wq, wk, wv, wo, wis, wus, *refs):
    shares, refs = refs[:9], refs[9:]
    out, ing, o1, oi, ou, osm, cnt = refs[:7]
    names = [a[0] for a in ACTS]
    for group in ("w1 wi wu", "sp bi sg sgi", "G R B C", "Dz E P1 Pi", "S CN cR cB", "cC cD M mR", "mB mC mD"):
        names += group.split()
    r = Refs()
    for n, ref in zip(names, refs[7:]):
        setattr(r, n, ref)
    r.sl, r.mol, r.og, r.out, r.ing = sl, mol, og, out, ing
    r.q, r.n2, r.gc = ing, out, r.gp.at[:, 2 * D : 3 * D]
    sem = list(refs[7 + len(names) :])
    free = sem.pop()
    sems = [(sem[2 * i], sem[2 * i + 1]) for i in range(len(sem) // 2)]
    row = lambda i, k: (sems[i][0].at[k], sems[i][1].at[k])
    h = Here()
    c = h.c
    r.slot = lambda g, half, s: jnp.where(half == c, 2 * g + s, 6 + s)

    peers = [h.partner, h.p, h.q] + h.zp
    bar = pltpu.get_barrier_semaphore()
    for d in peers:
        pl.semaphore_signal(bar, inc=1, device_id=d, device_id_type=MESH)
    pl.semaphore_wait(bar, len(peers))

    ex = Copies(h, sems[0])
    for k, w in enumerate((wq, wk, wv, wo)):
        ex.go(k, w, r.P1.at[k], h.partner)
    small = SmallGather(h, sems[1])
    small.one(r.S, shares)
    for s in range(2):
        ex.go(4 + s, wis.at[:, pl.ds(pl.multiple_of((2 * (1 - c) + s) * D, D), D)], r.Pi.at[s], h.partner)

    units = [Gather(h, row(2, s), lambda c, k, n, s=s: r.w1.at[2 * c + s, pl.ds(k, n)]) for s in range(2)]
    units += [Gather(h, row(2, 2 + s), lambda c, k, n, s=s: r.wi.at[2 * c + s, pl.ds(k, n)]) for s in range(2)]
    units += [Gather(h, row(2, 4 + s), lambda c, k, n, s=s: r.wu.at[pl.ds(k, n), 2 * c + s]) for s in range(2)]

    def join(mine, theirs):
        a, b = mine.astype(F32), theirs.astype(F32)
        return jnp.concatenate([jnp.where(c == 0, a, b), jnp.where(c == 0, b, a)], axis=0).astype(BF)

    for k in range(4):
        ex.wait(k, r.P1.at[k])
    small.two()
    pick = lambda a, b: jnp.where(c == 0, a.astype(F32), b.astype(F32))
    for s, (a, b) in enumerate(((wq, wv), (wk, wo))):
        r.w1[2 * c + s, h.chip] = join(pick(a[...], b[...]), pick(r.P1[s], r.P1[2 + s]))
        units[s].own()
    for s in range(2):
        ex.wait(4 + s, r.Pi.at[s])
        r.wi[2 * c + s, h.chip] = join(wis[:, pl.ds(pl.multiple_of((2 * c + s) * D, D), D)], r.Pi[s])
        units[2 + s].own()
    for s in range(2):
        r.wu[h.chip, 2 * c + s] = wus[48 * s : 48 * s + 48, :]
        units[4 + s].own()

    X = [[Sum(h, row(3, 2 * g + s), r.G.at[2 * g + s], r.R.at[s], r.B.at[2 * g + s], r.C.at[2 * g + s], r.Dz.at[2 * g + s])
          for s in range(2)] for g in range(3)]
    count = Sum(h, sems[4], r.CN.at[c], r.cR, r.cB, r.cC, r.cD)
    place = Gather(h, sems[5], lambda c, k, n: cnt.at[:, pl.ds(pl.multiple_of((c * 64 + k * 4) * 128, 512), n * 512)])
    msum = Sum(h, sems[6], r.M.at[c], r.mR, r.mB, r.mC, r.mD)

    def pair(g, s):
        if g:
            pl.semaphore_wait(free.at[s], 1)
        X[g][s].pair(r.G.at[6 + s])

    def paired(g, s):
        X[g][s].started.pop(0).wait_send()

    def first(g, s):
        X[g][s].first()
        if g < 2:
            pl.semaphore_signal(free.at[s], inc=1, device_id=h.partner, device_id_type=MESH)

    def last(g, s):
        x = X[g][s]
        if g == 0:
            ou[48 * s : 48 * s + 48, :] = x.total()
        else:
            split_rows(x, r.E.at[2 * (g - 1) + s], (oi if g == 1 else o1).at[2 * c + s])

    U = units
    histogram(ids, r.CN)
    count.pair(r.CN.at[1 - c])
    small.three()
    U[0].zrelay()
    small.four()
    count.first()
    U[1].zrelay()
    U[0].prelay()
    small.five()
    unpack(r.S, r.sp, r.bi)
    ln1(r)
    count.second()
    U[2].zrelay()
    U[1].prelay()
    U[0].qwait()
    count.third()
    U[3].zrelay()
    U[1].qwait()
    for s in range(2):
        U[s].fin()
    qkv(r)
    U[2].prelay()
    attn_fwd(r, 0, 3)
    U[4].zrelay()
    attn_fwd(r, 3, 6)
    outproj(r)
    ln2(r)
    U[2].qwait()
    U[2].fin()
    U[3].prelay()
    inner(r, 0)
    U[5].zrelay()
    U[3].qwait()
    U[3].fin()
    t = count.total()
    for k in range(4):
        cnt[:, pl.ds(pl.multiple_of((c * 64 + h.chip * 4 + k) * 128, 128), 128)] = t[8 * k : 8 * k + 8].astype(I32)
    U[4].prelay()
    inner(r, 1)
    pair(0, 0)
    pair(0, 1)
    U[4].qwait()
    U[5].prelay()
    first(0, 0)
    first(0, 1)
    grad_top_sum(r)
    U[5].qwait()
    for s in range(2):
        U[4 + s].fin()
    paired(0, 0)
    ginner(r, 0, 2)
    X[0][0].second()
    pair(1, 0)
    paired(0, 1)
    ginner(r, 1, 1)
    first(1, 0)
    X[0][1].second()
    ginner(r, 3, 1)
    pair(1, 1)
    X[0][0].third()
    gn2(r)
    first(1, 1)
    X[0][1].third()
    place.own()
    ln2b(r)
    paired(1, 0)
    paired(1, 1)
    gctx(r)
    X[1][0].second()
    attn_bwd(r, 0, 3)
    gw1(r, 0)
    pair(2, 0)
    X[1][1].second()
    X[1][0].third()
    place.zrelay()
    last(0, 0)
    attn_bwd(r, 3, 6)
    first(2, 0)
    gw1(r, 1)
    pair(2, 1)
    X[1][1].third()
    place.prelay()
    gn1(r)
    first(2, 1)
    ln1b(r)
    pack(r.sg, r.sgi, r.M)
    msum.pair(r.M.at[1 - c])
    X[2][0].second()
    place.qwait()
    msum.first()
    last(0, 1)
    X[2][0].third()
    X[2][1].second()
    msum.second()
    outp(r)
    X[2][1].third()
    msum.third()
    last(1, 0)
    last(1, 1)
    last(2, 0)
    last(2, 1)
    osm[...] = msum.total()
    place.fin()
    for g in (1, 2):
        for s in range(2):
            o = (oi if g == 1 else o1).at[2 * (1 - c) + s]
            X[g][s].wait(7, o)
    for k in [ex, small, place, count, msum] + units + [x for xs in X for x in xs]:
        k.drain()


def sems(*n):
    return [pltpu.SemaphoreType.DMA(n), pltpu.SemaphoreType.DMA(n)]


def layer_call(*args):
    S = jax.ShapeDtypeStruct
    V = lambda *s: pltpu.VMEM(s, BF)
    W = lambda *s: pltpu.VMEM(s, F32)
    return pl.pallas_call(
        layer_kernel,
        out_shape=[S((T, D), BF), S((T, D), BF), S((4, 24, D), F32), S((4, 24, D), F32), S((96, D), F32), S((8, 128), F32), S((8, BUCKETS), I32)],
        in_specs=[pl.BlockSpec(memory_space=pltpu.SMEM)] + [VM] * 18,
        out_specs=[VM] * 7,
        scratch_shapes=[pltpu.VMEM(s, d) for _, s, d in ACTS]
        + [V(4, 16, 48, D), V(4, 16, 48, D), V(16, 4, 48, D), W(8, D), W(1, FF), W(8, D), W(1, FF)]
        + [V(8, 16, 48, D), V(2, 16, 48, D), V(6, 2, 4, 48, D), V(6, 4, 48, D), V(6, 3, 48, D), W(4, 48, D)]
        + [V(4, 24, D), V(2, 24, D), W(32, 16, 128)]
        + [W(2, 16, 32, 128), W(16, 32, 128), W(2, 4, 32, 128), W(4, 32, 128), W(3, 32, 128)]
        + [W(2, 16, 8, 128), W(16, 8, 128), W(2, 4, 8, 128), W(4, 8, 128), W(3, 8, 128)]
        + sems(6) + sems(7) + sems(6, N_GATHER) + sems(6, N_SUM) + sems(N_SUM) + sems(N_GATHER) + sems(N_SUM)
        + [pltpu.SemaphoreType.REGULAR((2,))],
        compiler_params=pltpu.CompilerParams(collective_id=0, has_side_effects=True, vmem_limit_bytes=VMEM_BYTES),
    )(*args)


def finish_kernel(out, ing, o1, oi, ou, osm, cnt, *dst):
    dst[0][...] = out[...]
    dst[1][...] = ing[...]
    for k in range(4):
        for u in range(2):
            dst[2 + k][:, 384 * u : 384 * u + 384] = o1[2 * (k // 2) + u, :, 384 * (k % 2) : 384 * (k % 2) + 384]
        dst[6][:, D * k : D * k + D] = oi[k]
    dst[7][...] = ou[...]
    dst[8][...] = cnt[...]
    for j in range(8):
        dst[9 + j][...] = osm[j // 4 : j // 4 + 1, 32 * (j % 4) : 32 * (j % 4) + 24].reshape(24)
    dst[17][...] = osm[2:3, 0:96].reshape(96)


def finish_call(*args):
    S = lambda *s: jax.ShapeDtypeStruct(s, F32)
    return pl.pallas_call(
        finish_kernel,
        out_shape=[jax.ShapeDtypeStruct((T, D), BF)] * 2 + [S(24, D)] * 4 + [S(24, FF), S(96, D), jax.ShapeDtypeStruct((8, BUCKETS), I32)] + [S(24)] * 8 + [S(96)],
        in_specs=[VM] * 7,
        out_specs=[VM] * 18,
    )(*args)


def local(mol, lens, ids, og, *par):
    l1g, l1b, wq, bq, wk, wv, bv, wo, bo, l2g, l2b, wi, bi, wu, bu = par
    res = layer_call(lens, mol[0], og[0], ids, wq, wk, wv, wo, wi, wu, l1g, l1b, bq, bv, bo, l2g, l2b, bu, bi)
    out, ing, gq, gk, gv, go, gi, gu, cnt, *s = finish_call(*res)
    return (out[None], ing[None], s[0], s[1], gq, s[2], gk, gv, s[3], go, s[4], s[5], s[6], gi, s[8], gu, s[7], cnt)


def plain_kernel(sl, mol, og, sp, bi, w1, wi, wu, out, ing, G, sg, sgi, *acts):
    r = Refs()
    r.__dict__.update(sl=sl, mol=mol, og=og, sp=sp, bi=bi, w1=w1, wi=wi, wu=wu, out=out, ing=ing, G=G, sg=sg, sgi=sgi)
    for (n, _, _), ref in zip(ACTS, acts):
        setattr(r, n, ref)
    r.q, r.n2, r.gc = ing, out, r.gp.at[:, 2 * D : 3 * D]
    r.slot = lambda g, half, s: 4 * g + 2 * half + s
    ln1(r)
    qkv(r)
    attn_fwd(r, 0, PAIRS)
    outproj(r)
    ln2(r)
    inner(r, 0)
    inner(r, 1)
    grad_top_sum(r)
    ginner(r, 0, 2)
    ginner(r, 1, 2)
    gn2(r)
    ln2b(r)
    gctx(r)
    attn_bwd(r, 0, PAIRS)
    gw1(r, 0)
    gw1(r, 1)
    gn1(r)
    ln1b(r)
    outp(r)


def plain(mol, lens, ids, og, *par):
    a = ("dp", "fsdp")
    full = [lax.all_gather(p, a, axis=0, tiled=True) for p in par]
    l1g, l1b, wq, bq, wk, wv, bv, wo, bo, l2g, l2b, wi, bi, wu, bu = full
    S = jax.ShapeDtypeStruct
    sp = jnp.stack([l1g, l1b, bq, bv, bo, l2g, l2b, bu]).astype(F32)
    w1 = jnp.stack([wq, wk, wv, wo]).reshape(4, 16, 48, D)
    wi = wi.reshape(D, 4, D).transpose(1, 0, 2).reshape(4, 16, 48, D)
    out, ing, G, sg, sgi = pl.pallas_call(
        plain_kernel,
        out_shape=[S((T, D), BF), S((T, D), BF), S((12, 16, 48, D), BF), S((8, D), F32), S((1, FF), F32)],
        in_specs=[pl.BlockSpec(memory_space=pltpu.SMEM)] + [VM] * 7,
        out_specs=[VM] * 5,
        scratch_shapes=[pltpu.VMEM(s, d) for _, s, d in ACTS],
        compiler_params=pltpu.CompilerParams(vmem_limit_bytes=VMEM_BYTES),
    )(lens, mol[0], og[0], sp, bi.astype(F32)[None], w1, wi, wu.reshape(16, 4, 48, D))
    rs = lambda g: lax.psum_scatter(g.astype(F32), a, scatter_dimension=0, tiled=True)
    gu = rs(G[0:4].transpose(1, 0, 2, 3).reshape(FF, D))
    gi = rs(G[4:8].reshape(4, D, D).transpose(1, 0, 2).reshape(D, FF))
    g1 = G[8:12].reshape(2, 2, D, 2, 384).transpose(0, 3, 2, 1, 4).reshape(4, D, D)
    w = [rs(g1[k]) for k in range(4)]
    s = [rs(sg[k]) for k in range(8)]
    hist = pl.pallas_call(
        histogram, out_shape=S((2, 16, 32, 128), F32), in_specs=[VM], out_specs=VM
    )(ids)
    cnt = lax.psum(hist, a).reshape(128, 8, 128).transpose(1, 0, 2).reshape(8, BUCKETS).astype(I32)
    return (out[None], ing[None], s[0], s[1], w[0], s[2], w[1], w[2], s[3], w[3], s[4], s[5], s[6], gi, rs(sgi[0]), gu, s[7], cnt)


def solution(mesh):
    a = ("dp", "fsdp")
    r, r2, r3 = P(a), P(a, None), P(a, None, None)
    in_specs = (r3, r, P(None, a), r3, r, r, r2, r, r2, r2, r, r2, r, r, r, r2, r, r2, r)
    out_specs = (r3, r3, r, r, r2, r, r2, r2, r, r2, r, r, r, r2, r, r2, r, P())
    body = local if dict(mesh.shape) == {"dp": 4, "fsdp": 8} else plain
    return jax.shard_map(body, mesh=mesh, in_specs=in_specs, out_specs=out_specs, check_vma=False)
```

```python
import functools

import jax
import jax.numpy as jnp
from jax import lax
from jax.experimental import pallas as pl
from jax.experimental.pallas import tpu as pltpu
from jax.sharding import PartitionSpec as P

F32 = jnp.float32
BF = jnp.bfloat16
I32 = jnp.int32
MESH = pl.DeviceIdType.MESH
VM = pl.BlockSpec(memory_space=pltpu.VMEM)
EPS = 1e-5
RSQRT2 = 0.7071067811865476
RSQRT2PI = 0.3989422804014327
VMEM_BYTES = 67043328
T, D, FF, PAIRS, BUCKETS = 512, 768, 3072, 6, 16384
ROWT = 128
CT = 256


def mm(a, b):
    return lax.dot_general(a, b, (((1,), (0,)), ((), ())), preferred_element_type=F32)


def nt(a, b):
    return lax.dot_general(a, b, (((1,), (1,)), ((), ())), preferred_element_type=F32)


def tn(a, b):
    return lax.dot_general(a, b, (((0,), (0,)), ((), ())), preferred_element_type=F32)


def at(i, n):
    return pl.multiple_of(i * n, n)


def ds(i, n):
    return pl.ds(at(i, n), n)


def loop(n, body):
    def step(i, carry):
        body(i)
        return carry

    lax.fori_loop(0, n, step, 0)


def norm_rows(v):
    cen = v - jnp.mean(v, axis=-1, keepdims=True)
    r = lax.rsqrt(jnp.mean(cen * cen, axis=-1, keepdims=True) + EPS)
    return cen * r, r


def ln1(r):
    g, b = r.sp[0:1, :], r.sp[1:2, :]

    def body(i):
        n, _ = norm_rows(r.mol[ds(i, ROWT), :].astype(F32))
        r.nrm[ds(i, ROWT), :] = (n * g + b).astype(BF)

    loop(T // ROWT, body)


def qkv(r):
    def body(j):
        n = r.nrm[...]
        c = ds(j, CT)
        w = lambda m: r.w1[m, :, :, c].reshape(D, CT)
        q = mm(n, w(0)) + r.sp[2:3, c]
        r.q[:, c] = (q.astype(BF).astype(F32) * 0.125).astype(BF)
        r.k[:, c] = mm(n, w(1)).astype(BF)
        r.v[:, c] = (mm(n, w(2)) + r.sp[3:4, c]).astype(BF)

    loop(D // CT, body)


def low_half():
    return lax.broadcasted_iota(I32, (1, 128), 1) < 64


def attn_fwd(r, first, last):
    def body(j):
        lo = low_half()
        kpos = lax.broadcasted_iota(I32, (T, 128), 0)
        bias = jnp.where(kpos < r.sl[0], 0.0, -1e30 / 64).astype(BF)
        c = ds(j + first, 128)
        q2, k2, v2 = r.q[:, c], r.k[:, c], r.v[:, c]
        one = jnp.ones((), BF)
        outs = []
        for h in (0, 1):
            half = lo if h == 0 else jnp.logical_not(lo)
            s = nt(jnp.where(half, q2, one), jnp.where(half, k2, bias))
            p = jnp.exp(s - jnp.max(s, axis=-1, keepdims=True)).astype(BF)
            r.p[2 * (j + first) + h] = p
            outs.append(mm(p, jnp.where(half, v2, one)))
        rl = 1.0 / pltpu.roll(jnp.where(lo, outs[1], outs[0]), 64, 1)
        r.rl[:, c] = rl
        r.ctx[:, c] = (jnp.where(lo, outs[0], outs[1]) * rl).astype(BF)

    loop(last - first, body)


def outproj(r):
    def body(j):
        c = ds(j, CT)
        r.mid[:, c] = r.mol[:, c].astype(F32) + (
            mm(r.ctx[...], r.w1[3, :, :, c].reshape(D, CT)) + r.sp[4:5, c]
        )

    loop(D // CT, body)


def ln2(r):
    g, b = r.sp[5:6, :], r.sp[6:7, :]

    def body(i):
        n, _ = norm_rows(r.mid[ds(i, ROWT), :])
        v = n * g + b
        r.n2T[:, ds(i, ROWT)] = v.T.astype(BF)
        r.n2[ds(i, ROWT), :] = v.astype(BF)

    loop(T // ROWT, body)


def inner(r, s):
    def body(i):
        j = i + 2 * (i // 2) + 2 * s
        c = ds(j, 384)
        w = r.wi[j // 2, :, :, ds(lax.rem(j, 2), 384)].reshape(D, 384)
        u = mm(r.n2[...], w) + r.bi[0:1, c]
        ph = 0.5 + 0.5 * lax.erf(u * RSQRT2)
        hid = (u * ph).astype(BF)
        r.hid[:, c] = hid
        r.gp[:, c] = (ph + u * (RSQRT2PI * jnp.exp(-0.5 * u * u))).astype(BF)
        t = tn(hid, r.og[...]).astype(BF).reshape(2, 4, 48, D)
        for k in range(4):
            r.G[r.slot(0, k // 2, k % 2), pl.ds(2 * j, 2)] = t[:, k]

    loop(4, body)


def grad_top_sum(r):
    def body(i, a):
        return a + jnp.sum(r.og[ds(i, ROWT), :].astype(F32), axis=0, keepdims=True)

    r.sg[7:8, :] = lax.fori_loop(0, T // ROWT, body, jnp.zeros((1, D), F32))


def outp(r):
    def body(j):
        c = ds(j, CT)
        w = r.wu[:, :, :, c].reshape(FF, CT)
        low = pl.ds(pl.multiple_of(D + j * CT, CT), CT)
        mid = r.gp[:, c].astype(F32) + r.gp[:, low].astype(F32)
        r.out[:, c] = (mid + (mm(r.hid[...], w) + r.sp[7:8, c])).astype(BF)

    loop(D // CT, body)


def ginner(r, first, n):
    def body(k):
        i = first + 2 * k
        w = r.wu[ds(i, 4)].reshape(D, D)
        for t in range(3):
            c = pl.ds(pl.multiple_of(i * D + CT * t, CT), CT)
            gi = nt(r.og[...], w[CT * t : CT * t + CT]) * r.gp[:, c].astype(F32)
            r.sgi[0:1, c] = jnp.sum(gi, axis=0, keepdims=True)
            gib = gi.astype(BF)
            r.gp[:, c] = gib
            r.G[r.slot(1, i // 2, lax.rem(i, 2)), :, :, CT * t : CT * t + CT] = (
                mm(r.n2T[...], gib).astype(BF).reshape(16, 48, CT)
            )

    loop(n, body)


def gn2(r):
    def body(j):
        e = None
        for i in range(4):
            w = r.wi[i, pl.ds(8 * j, 8)].reshape(384, D)
            t = nt(r.gp[:, D * i : D * i + D], w)
            e = t if e is None else e + t
        r.e[:, ds(j, 384)] = e

    loop(2, body)


def ln_bwd(r, src, gain_row, first):
    gain = r.sp[gain_row : gain_row + 1, :]

    def body(i, a):
        rows = ds(i, ROWT)
        v = src[rows, :].astype(F32)
        n, rs = norm_rows(v)
        e = r.e[rows, :]
        eg = e * gain
        m1 = jnp.mean(eg, axis=-1, keepdims=True)
        m2 = jnp.mean(eg * n, axis=-1, keepdims=True)
        gv = rs * (eg - m1 - n * m2)
        a0 = a[0] + jnp.sum(e * n, axis=0, keepdims=True)
        a1 = a[1] + jnp.sum(e, axis=0, keepdims=True)
        if first:
            r.ing[rows, :] = (r.mid[rows, :] + gv).astype(BF)
            return (a0, a1)
        gm = r.og[rows, :].astype(F32) + gv
        hi = v.astype(BF)
        r.gp[rows, 0:D] = hi
        r.gp[rows, D : 2 * D] = (v - hi.astype(F32)).astype(BF)
        r.mid[rows, :] = gm
        r.n2[rows, :] = gm.astype(BF)
        return (a0, a1, a[2] + jnp.sum(gm, axis=0, keepdims=True))

    z = jnp.zeros((1, D), F32)
    return lax.fori_loop(0, T // ROWT, body, (z, z) if first else (z, z, z))


def ln2b(r):
    a = ln_bwd(r, r.mid, 5, False)
    r.sg[5:6, :] = a[0]
    r.sg[6:7, :] = a[1]
    r.sg[4:5, :] = a[2]


def gctx(r):
    def body(j):
        c = ds(j, 384)
        k = pl.ds(8 * j, 8)
        g = tn(r.ctx[:, c], r.n2[...]).astype(BF).reshape(8, 48, D)
        for s in range(2):
            r.G[r.slot(2, 1, s), k, :, 384:768] = g[:, :, 384 * s : 384 * s + 384]
        r.gc[:, c] = nt(r.n2[...], r.w1[3, k].reshape(384, D)).astype(BF)

    loop(2, body)


def attn_bwd(r, first, last):
    def body(j):
        lo = low_half()
        c = ds(j + first, 128)
        q2, k2, v2 = r.q[:, c], r.k[:, c], r.v[:, c]
        gp = r.gc[:, c].astype(F32) * r.rl[:, c]
        dd = r.ctx[:, c].astype(F32) * gp
        gpb = gp.astype(BF)
        zero = jnp.zeros((), BF)
        gT = gp.T.astype(BF)
        qT = q2.astype(F32).T.astype(BF)
        dq, dkT, dvT = [], [], []
        for h in (0, 1):
            half = lo if h == 0 else jnp.logical_not(lo)
            dsum = jnp.sum(jnp.where(half, dd, 0.0), axis=-1, keepdims=True)
            dp = nt(jnp.where(half, gpb, zero), v2)
            p = r.p[2 * (j + first) + h]
            dsl = (p.astype(F32) * (dp - dsum)).astype(BF)
            dq.append(mm(dsl, k2))
            dvT.append(mm(gT[64 * h : 64 * h + 64], p))
            dkT.append(mm(qT[64 * h : 64 * h + 64], dsl))
        gq = jnp.where(lo, dq[0], dq[1]) * 0.125
        gv = jnp.concatenate(dvT, axis=0).T
        gk = jnp.concatenate(dkT, axis=0).T
        r.sg[2:3, c] = jnp.sum(gq, axis=0, keepdims=True)
        r.sg[3:4, c] = jnp.sum(gv, axis=0, keepdims=True)
        r.gc[:, c] = gq.astype(BF)
        r.k[:, c] = gk.astype(BF)
        r.v[:, c] = gv.astype(BF)

    loop(last - first, body)


def gw1(r, s):
    def body(j):
        n = r.nrm[:, ds(j, 384)]
        k = pl.ds(8 * j, 8)
        for h, t, g in ((0, 0, r.gc), (0, 384, r.k), (1, 0, r.v)):
            d = tn(n, g[:, 384 * s : 384 * s + 384]).astype(BF)
            r.G[r.slot(2, h, s), k, :, t : t + 384] = d.reshape(8, 48, 384)

    loop(2, body)


def gn1(r):
    def body(j):
        k = pl.ds(8 * j, 8)
        e = None
        for m, g in enumerate((r.gc, r.k, r.v)):
            t = nt(g[...], r.w1[m, k].reshape(384, D))
            e = t if e is None else e + t
        r.e[:, ds(j, 384)] = e

    loop(2, body)


def ln1b(r):
    a = ln_bwd(r, r.mol, 0, True)
    r.sg[0:1, :] = a[0]
    r.sg[1:2, :] = a[1]


ACTS = [
    ("nrm", (T, D), BF), ("k", (T, D), BF), ("v", (T, D), BF), ("p", (12, T, T), BF),
    ("rl", (T, D), F32), ("ctx", (T, D), BF), ("mid", (T, D), F32), ("n2T", (D, T), BF),
    ("hid", (T, FF), BF), ("gp", (T, FF), BF), ("e", (T, D), F32),
]


class Refs:
    pass


def histogram(ids, CN):
    i = lax.broadcasted_iota(I32, (128, 1), 0)

    def body(k):
        v = ids[pl.ds(k, 1), :]
        hi = jnp.where(i == lax.shift_right_logical(v, 7), 1.0, 0.0).astype(BF)
        lo = jnp.where(i == jnp.bitwise_and(v, 127), 1.0, 0.0).astype(BF)
        c = nt(hi, lo)
        for half in range(2):
            for q in range(16):
                m = 64 * half + 4 * q
                CN[half, q, pl.ds(k, 4, stride=8), :] = c[m : m + 4]

    loop(8, body)


class Here:
    def __init__(s):
        dp, fs = lax.axis_index("dp"), lax.axis_index("fsdp")
        s.y, s.x, s.z, s.c = y, x, z, c = dp // 2, dp % 2, fs // 2, fs % 2
        dev = lambda y, x, z, c: (y * 2 + x, z * 2 + c)
        py, px = jnp.where(c == 0, y, 1 - y), jnp.where(c == 0, 1 - x, x)
        qy, qx = jnp.where(c == 0, 1 - y, y), jnp.where(c == 0, x, 1 - x)
        s.partner, s.p, s.q = dev(y, x, z, 1 - c), dev(py, px, z, c), dev(qy, qx, z, c)
        s.zp = [dev(y, x, lax.rem(z + d, 4), c) for d in (1, 2, 3)]
        s.line, s.pline, s.qline, s.pqline = y * 2 + x, py * 2 + px, qy * 2 + qx, (1 - y) * 2 + (1 - x)
        s.chip = s.line * 4 + s.z

    def before(s, line, d):
        return line * 4 + lax.rem(s.z + 4 - d, 4)

    def start4(s, i, away):
        y, x = jnp.where(away, 1 - s.y, s.y), jnp.where(away, 1 - s.x, s.x)
        return jnp.where(s.c == 0, y * 2 + i, i * 2 + x) * 4

    def keep(s):
        return jnp.where(s.c == 0, s.x, s.y)


class Copies:
    def __init__(s, h, sems):
        s.h, (s.ss, s.rs), s.started = h, sems, []

    def copy(s, i, src, dst, dev):
        return pltpu.make_async_remote_copy(
            src_ref=src, dst_ref=dst, send_sem=s.ss.at[i], recv_sem=s.rs.at[i], device_id=dev, device_id_type=MESH
        )

    def go(s, i, src, dst, dev):
        cp = s.copy(i, src, dst, dev)
        cp.start()
        s.started.append(cp)

    def wait(s, i, dst):
        s.copy(i, dst, dst, s.h.partner).wait_recv()

    def drain(s):
        for cp in s.started:
            cp.wait_send()


class Gather(Copies):
    def __init__(s, h, sems, blk):
        super().__init__(h, sems)
        s.blk = blk

    def send(s, i, k, n, dev):
        b = s.blk(s.h.c, k, n)
        s.go(i, b, b, dev)

    def come(s, i, k):
        s.wait(i, s.blk(s.h.c, k, 1))

    def own(s):
        h = s.h
        for d in (1, 2, 3):
            s.send(d - 1, h.chip, 1, h.zp[d - 1])
        s.send(7, h.chip, 1, h.q)
        s.send(3, h.chip, 1, h.p)

    def zrelay(s):
        h = s.h
        for d in (1, 2, 3):
            k = h.before(h.line, d)
            s.come(d - 1, k)
            s.send(7 + d, k, 1, h.q)
            s.send(3 + d, k, 1, h.p)
        s.send(15, h.line * 4, 4, h.partner)

    def prelay(s):
        h = s.h
        for d in range(4):
            k = h.before(h.pline, d)
            s.come(3 + d, k)
            s.send(11 + d, k, 1, h.q)
        s.send(16, h.pline * 4, 4, h.partner)

    def qwait(s):
        h = s.h
        for base, line, i in ((7, h.qline, 17), (11, h.pqline, 18)):
            for d in range(4):
                s.come(base + d, h.before(line, d))
            s.send(i, line * 4, 4, h.partner)

    def fin(s):
        h = s.h
        for i, line in ((15, h.line), (16, h.pline), (17, h.qline), (18, h.pqline)):
            s.wait(i, s.blk(1 - h.c, line * 4, 4))


class Sum(Copies):
    def __init__(s, h, sems, V, R, B, C, Dz):
        super().__init__(h, sems)
        s.V, s.R, s.B, s.C, s.Dz = V, R, B, C, Dz

    def pair(s, src):
        s.go(0, src, s.R, s.h.partner)

    def add(s, k, src):
        for i in range(4):
            s.V[k + i] = s.V[k + i] + src[i]

    def first(s):
        h = s.h
        s.wait(0, s.R)
        for i in (0, 1):
            k = h.start4(i, True)
            s.add(k, s.R.at[pl.ds(k, 4)])
            s.go(1 + i, s.V.at[pl.ds(k, 4)], s.B.at[i], h.q)
        for i in (0, 1):
            k = h.start4(i, False)
            s.add(k, s.R.at[pl.ds(k, 4)])

    def second(s):
        h = s.h
        for i in (0, 1):
            s.wait(1 + i, s.B.at[i])
        i = 1 - h.keep()
        k = h.start4(i, False)
        s.add(k, s.B.at[i])
        s.go(3, s.V.at[pl.ds(k, 4)], s.C, h.p)
        s.add(h.start4(1 - i, False), s.B.at[1 - i])

    def third(s):
        h = s.h
        s.wait(3, s.C)
        k = h.start4(h.keep(), False)
        s.add(k, s.C)
        for d in (1, 2, 3):
            s.go(3 + d, s.V.at[pl.ds(k + lax.rem(h.z + d, 4), 1)], s.Dz.at[pl.ds(d - 1, 1)], h.zp[d - 1])

    def total(s):
        h = s.h
        t = s.V[h.start4(h.keep(), False) + h.z].astype(F32)
        for d in (1, 2, 3):
            s.wait(3 + d, s.Dz.at[pl.ds(d - 1, 1)])
            t = t + s.Dz[d - 1].astype(F32)
        return t


def split_rows(s, E, O):
    c = s.h.c
    E[...] = s.total()
    s.go(7, E.at[ds(1 - c, 24)], O, s.h.partner)
    O[...] = E[ds(c, 24), :]


class SmallGather(Copies):
    def send(s, i, k, n, dev):
        b = s.S.at[pl.ds(k, n)]
        s.go(i, b, b, dev)

    def come(s, i, k, n):
        s.wait(i, s.S.at[pl.ds(k, n)])

    def one(s, S, shares):
        h = s.h
        s.S, me = S, h.chip * 2 + h.c
        S[me] = jnp.zeros((16, 128), F32)
        for j, p in enumerate(shares):
            n = p.shape[0]
            S[me, j : j + 1, 0:n] = p[...].astype(F32).reshape(1, n)
        s.send(0, me, 1, h.partner)

    def two(s):
        h = s.h
        s.come(0, h.chip * 2 + 1 - h.c, 1)
        for d in (1, 2, 3):
            s.send(d, h.chip * 2, 2, h.zp[d - 1])

    def three(s):
        h = s.h
        for d in (1, 2, 3):
            s.come(d, h.before(h.line, d) * 2, 2)
        s.send(4, h.line * 8, 8, h.p)
        s.send(5, h.line * 8, 8, h.q)

    def four(s):
        h = s.h
        s.come(4, h.pline * 8, 8)
        s.send(6, h.pline * 8, 8, h.q)

    def five(s):
        h = s.h
        s.come(5, h.qline * 8, 8)
        s.come(6, h.pqline * 8, 8)


def share_mask(rows, width, base):
    n = lax.broadcasted_iota(I32, (rows, D), 1) + base
    return lax.rem(n, width) == lax.broadcasted_iota(I32, (rows, D), 0)


def owner_mask(width, base, by_core):
    d = lax.broadcasted_iota(I32, (32, D), 0)
    if by_core:
        d = lax.rem(d, 16) * 2 + d // 16
    n = lax.broadcasted_iota(I32, (32, D), 1) + base
    return jnp.logical_and(n >= d * width, n < d * width + width).astype(F32)


def unpack(S, sp, bi):
    keep, own = share_mask(24, 24, 0), owner_mask(24, 0, False).astype(BF)
    for j in range(8):
        u = tn(S[:, j, :].astype(BF), own)
        sp[j : j + 1, :] = jnp.sum(jnp.where(keep, u[0:24], 0.0), axis=0, keepdims=True)
    t = S[:, 8, :].astype(BF)
    for k in range(4):
        u = tn(t, owner_mask(96, D * k, False).astype(BF))
        bi[0:1, D * k : D * k + D] = jnp.sum(
            jnp.where(share_mask(96, 96, D * k), u[0:96], 0.0), axis=0, keepdims=True
        )


def pack(sg, sgi, M):
    dot = lambda a, b: lax.dot_general(
        a, b, (((1,), (1,)), ((), ())), precision=lax.Precision.HIGHEST, preferred_element_type=F32
    )
    keep, own = share_mask(32, 24, 0), owner_mask(24, 0, True)
    rows = []
    for half in range(2):
        y = [jnp.where(keep, sg[4 * half + j : 4 * half + j + 1, :], 0.0) for j in range(4)]
        rows.append(dot(own, jnp.concatenate(y, axis=0)))
    t = None
    for k in range(4):
        y = jnp.where(share_mask(128, 96, D * k), sgi[0:1, D * k : D * k + D], 0.0)
        u = dot(owner_mask(96, D * k, True), y)
        t = u if t is None else t + u
    rows.append(t)
    for i, m in enumerate(rows):
        for c in range(2):
            M[c, :, i, :] = m[16 * c : 16 * c + 16]


N_GATHER, N_SUM = 19, 8


def layer_kernel(sl, mol, og, ids, wq, wk, wv, wo, wis, wus, *refs):
    shares, refs = refs[:9], refs[9:]
    out, ing, o1, oi, ou, osm, cnt = refs[:7]
    names = [a[0] for a in ACTS]
    for group in ("w1 wi wu", "sp bi sg sgi", "G R B C", "Dz E P1 Pi", "S CN cR cB", "cC cD M mR", "mB mC mD"):
        names += group.split()
    r = Refs()
    for n, ref in zip(names, refs[7:]):
        setattr(r, n, ref)
    r.sl, r.mol, r.og, r.out, r.ing = sl, mol, og, out, ing
    r.q, r.n2, r.gc = ing, out, r.gp.at[:, 2 * D : 3 * D]
    sem = list(refs[7 + len(names) :])
    free = sem.pop()
    sems = [(sem[2 * i], sem[2 * i + 1]) for i in range(len(sem) // 2)]
    row = lambda i, k: (sems[i][0].at[k], sems[i][1].at[k])
    h = Here()
    c = h.c
    r.slot = lambda g, half, s: jnp.where(half == c, 2 * g + s, 6 + s)

    peers = [h.partner, h.p, h.q] + h.zp
    bar = pltpu.get_barrier_semaphore()
    for d in peers:
        pl.semaphore_signal(bar, inc=1, device_id=d, device_id_type=MESH)
    pl.semaphore_wait(bar, len(peers))

    ex = Copies(h, sems[0])
    for k, w in enumerate((wq, wk, wv, wo)):
        ex.go(k, w, r.P1.at[k], h.partner)
    small = SmallGather(h, sems[1])
    small.one(r.S, shares)
    for s in range(2):
        ex.go(4 + s, wis.at[:, pl.ds(pl.multiple_of((2 * (1 - c) + s) * D, D), D)], r.Pi.at[s], h.partner)

    units = [Gather(h, row(2, s), lambda c, k, n, s=s: r.w1.at[2 * c + s, pl.ds(k, n)]) for s in range(2)]
    units += [Gather(h, row(2, 2 + s), lambda c, k, n, s=s: r.wi.at[2 * c + s, pl.ds(k, n)]) for s in range(2)]
    units += [Gather(h, row(2, 4 + s), lambda c, k, n, s=s: r.wu.at[pl.ds(k, n), 2 * c + s]) for s in range(2)]

    def join(mine, theirs):
        a, b = mine.astype(F32), theirs.astype(F32)
        return jnp.concatenate([jnp.where(c == 0, a, b), jnp.where(c == 0, b, a)], axis=0).astype(BF)

    for k in range(4):
        ex.wait(k, r.P1.at[k])
    small.two()
    pick = lambda a, b: jnp.where(c == 0, a.astype(F32), b.astype(F32))
    for s, (a, b) in enumerate(((wq, wv), (wk, wo))):
        r.w1[2 * c + s, h.chip] = join(pick(a[...], b[...]), pick(r.P1[s], r.P1[2 + s]))
        units[s].own()
    for s in range(2):
        ex.wait(4 + s, r.Pi.at[s])
        r.wi[2 * c + s, h.chip] = join(wis[:, pl.ds(pl.multiple_of((2 * c + s) * D, D), D)], r.Pi[s])
        units[2 + s].own()
    for s in range(2):
        r.wu[h.chip, 2 * c + s] = wus[48 * s : 48 * s + 48, :]
        units[4 + s].own()

    X = [[Sum(h, row(3, 2 * g + s), r.G.at[2 * g + s], r.R.at[s], r.B.at[2 * g + s], r.C.at[2 * g + s], r.Dz.at[2 * g + s])
          for s in range(2)] for g in range(3)]
    count = Sum(h, sems[4], r.CN.at[c], r.cR, r.cB, r.cC, r.cD)
    place = Gather(h, sems[5], lambda c, k, n: cnt.at[:, pl.ds(pl.multiple_of((c * 64 + k * 4) * 128, 512), n * 512)])
    msum = Sum(h, sems[6], r.M.at[c], r.mR, r.mB, r.mC, r.mD)

    def pair(g, s):
        if g:
            pl.semaphore_wait(free.at[s], 1)
        X[g][s].pair(r.G.at[6 + s])

    def paired(g, s):
        X[g][s].started.pop(0).wait_send()

    def first(g, s):
        X[g][s].first()
        if g < 2:
            pl.semaphore_signal(free.at[s], inc=1, device_id=h.partner, device_id_type=MESH)

    def last(g, s):
        x = X[g][s]
        if g == 0:
            ou[48 * s : 48 * s + 48, :] = x.total()
        else:
            split_rows(x, r.E.at[2 * (g - 1) + s], (oi if g == 1 else o1).at[2 * c + s])

    U = units
    histogram(ids, r.CN)
    count.pair(r.CN.at[1 - c])
    small.three()
    U[0].zrelay()
    small.four()
    count.first()
    U[1].zrelay()
    U[0].prelay()
    small.five()
    unpack(r.S, r.sp, r.bi)
    ln1(r)
    count.second()
    U[2].zrelay()
    U[1].prelay()
    count.third()
    U[3].zrelay()
    U[0].qwait()
    U[1].qwait()
    for s in range(2):
        U[s].fin()
    U[2].prelay()
    U[4].zrelay()
    qkv(r)
    U[5].zrelay()
    attn_fwd(r, 0, 3)
    U[3].prelay()
    attn_fwd(r, 3, 6)
    outproj(r)
    ln2(r)
    U[2].qwait()
    U[2].fin()
    inner(r, 0)
    U[3].qwait()
    U[3].fin()
    t = count.total()
    for k in range(4):
        cnt[:, pl.ds(pl.multiple_of((c * 64 + h.chip * 4 + k) * 128, 128), 128)] = t[8 * k : 8 * k + 8].astype(I32)
    U[4].prelay()
    U[5].prelay()
    inner(r, 1)
    pair(0, 0)
    pair(0, 1)
    U[4].qwait()
    first(0, 0)
    first(0, 1)
    grad_top_sum(r)
    U[5].qwait()
    for s in range(2):
        U[4 + s].fin()
    paired(0, 0)
    ginner(r, 0, 2)
    X[0][0].second()
    pair(1, 0)
    paired(0, 1)
    ginner(r, 1, 1)
    first(1, 0)
    X[0][1].second()
    ginner(r, 3, 1)
    pair(1, 1)
    X[0][0].third()
    gn2(r)
    first(1, 1)
    X[0][1].third()
    place.own()
    ln2b(r)
    paired(1, 0)
    paired(1, 1)
    gctx(r)
    X[1][0].second()
    attn_bwd(r, 0, 3)
    gw1(r, 0)
    pair(2, 0)
    X[1][1].second()
    X[1][0].third()
    place.zrelay()
    last(0, 0)
    attn_bwd(r, 3, 6)
    first(2, 0)
    gw1(r, 1)
    pair(2, 1)
    X[1][1].third()
    place.prelay()
    gn1(r)
    first(2, 1)
    ln1b(r)
    pack(r.sg, r.sgi, r.M)
    msum.pair(r.M.at[1 - c])
    X[2][0].second()
    place.qwait()
    msum.first()
    last(0, 1)
    X[2][0].third()
    X[2][1].second()
    msum.second()
    outp(r)
    X[2][1].third()
    msum.third()
    last(1, 0)
    last(1, 1)
    last(2, 0)
    last(2, 1)
    osm[...] = msum.total()
    place.fin()
    for g in (1, 2):
        for s in range(2):
            o = (oi if g == 1 else o1).at[2 * (1 - c) + s]
            X[g][s].wait(7, o)
    for k in [ex, small, place, count, msum] + units + [x for xs in X for x in xs]:
        k.drain()


def sems(*n):
    return [pltpu.SemaphoreType.DMA(n), pltpu.SemaphoreType.DMA(n)]


def layer_call(*args):
    S = jax.ShapeDtypeStruct
    V = lambda *s: pltpu.VMEM(s, BF)
    W = lambda *s: pltpu.VMEM(s, F32)
    return pl.pallas_call(
        layer_kernel,
        out_shape=[S((T, D), BF), S((T, D), BF), S((4, 24, D), F32), S((4, 24, D), F32), S((96, D), F32), S((8, 128), F32), S((8, BUCKETS), I32)],
        in_specs=[pl.BlockSpec(memory_space=pltpu.SMEM)] + [VM] * 18,
        out_specs=[VM] * 7,
        scratch_shapes=[pltpu.VMEM(s, d) for _, s, d in ACTS]
        + [V(4, 16, 48, D), V(4, 16, 48, D), V(16, 4, 48, D), W(8, D), W(1, FF), W(8, D), W(1, FF)]
        + [V(8, 16, 48, D), V(2, 16, 48, D), V(6, 2, 4, 48, D), V(6, 4, 48, D), V(6, 3, 48, D), W(4, 48, D)]
        + [V(4, 24, D), V(2, 24, D), W(32, 16, 128)]
        + [W(2, 16, 32, 128), W(16, 32, 128), W(2, 4, 32, 128), W(4, 32, 128), W(3, 32, 128)]
        + [W(2, 16, 8, 128), W(16, 8, 128), W(2, 4, 8, 128), W(4, 8, 128), W(3, 8, 128)]
        + sems(6) + sems(7) + sems(6, N_GATHER) + sems(6, N_SUM) + sems(N_SUM) + sems(N_GATHER) + sems(N_SUM)
        + [pltpu.SemaphoreType.REGULAR((2,))],
        compiler_params=pltpu.CompilerParams(collective_id=0, has_side_effects=True, vmem_limit_bytes=VMEM_BYTES),
    )(*args)


def finish_kernel(out, ing, o1, oi, ou, osm, cnt, *dst):
    dst[0][...] = out[...]
    dst[1][...] = ing[...]
    for k in range(4):
        for u in range(2):
            dst[2 + k][:, 384 * u : 384 * u + 384] = o1[2 * (k // 2) + u, :, 384 * (k % 2) : 384 * (k % 2) + 384]
        dst[6][:, D * k : D * k + D] = oi[k]
    dst[7][...] = ou[...]
    dst[8][...] = cnt[...]
    for j in range(8):
        dst[9 + j][...] = osm[j // 4 : j // 4 + 1, 32 * (j % 4) : 32 * (j % 4) + 24].reshape(24)
    dst[17][...] = osm[2:3, 0:96].reshape(96)


def finish_call(*args):
    S = lambda *s: jax.ShapeDtypeStruct(s, F32)
    return pl.pallas_call(
        finish_kernel,
        out_shape=[jax.ShapeDtypeStruct((T, D), BF)] * 2 + [S(24, D)] * 4 + [S(24, FF), S(96, D), jax.ShapeDtypeStruct((8, BUCKETS), I32)] + [S(24)] * 8 + [S(96)],
        in_specs=[VM] * 7,
        out_specs=[VM] * 18,
    )(*args)


def local(mol, lens, ids, og, *par):
    l1g, l1b, wq, bq, wk, wv, bv, wo, bo, l2g, l2b, wi, bi, wu, bu = par
    res = layer_call(lens, mol[0], og[0], ids, wq, wk, wv, wo, wi, wu, l1g, l1b, bq, bv, bo, l2g, l2b, bu, bi)
    out, ing, gq, gk, gv, go, gi, gu, cnt, *s = finish_call(*res)
    return (out[None], ing[None], s[0], s[1], gq, s[2], gk, gv, s[3], go, s[4], s[5], s[6], gi, s[8], gu, s[7], cnt)


def plain_kernel(sl, mol, og, sp, bi, w1, wi, wu, out, ing, G, sg, sgi, *acts):
    r = Refs()
    r.__dict__.update(sl=sl, mol=mol, og=og, sp=sp, bi=bi, w1=w1, wi=wi, wu=wu, out=out, ing=ing, G=G, sg=sg, sgi=sgi)
    for (n, _, _), ref in zip(ACTS, acts):
        setattr(r, n, ref)
    r.q, r.n2, r.gc = ing, out, r.gp.at[:, 2 * D : 3 * D]
    r.slot = lambda g, half, s: 4 * g + 2 * half + s
    ln1(r)
    qkv(r)
    attn_fwd(r, 0, PAIRS)
    outproj(r)
    ln2(r)
    inner(r, 0)
    inner(r, 1)
    grad_top_sum(r)
    ginner(r, 0, 2)
    ginner(r, 1, 2)
    gn2(r)
    ln2b(r)
    gctx(r)
    attn_bwd(r, 0, PAIRS)
    gw1(r, 0)
    gw1(r, 1)
    gn1(r)
    ln1b(r)
    outp(r)


def plain(mol, lens, ids, og, *par):
    a = ("dp", "fsdp")
    full = [lax.all_gather(p, a, axis=0, tiled=True) for p in par]
    l1g, l1b, wq, bq, wk, wv, bv, wo, bo, l2g, l2b, wi, bi, wu, bu = full
    S = jax.ShapeDtypeStruct
    sp = jnp.stack([l1g, l1b, bq, bv, bo, l2g, l2b, bu]).astype(F32)
    w1 = jnp.stack([wq, wk, wv, wo]).reshape(4, 16, 48, D)
    wi = wi.reshape(D, 4, D).transpose(1, 0, 2).reshape(4, 16, 48, D)
    out, ing, G, sg, sgi = pl.pallas_call(
        plain_kernel,
        out_shape=[S((T, D), BF), S((T, D), BF), S((12, 16, 48, D), BF), S((8, D), F32), S((1, FF), F32)],
        in_specs=[pl.BlockSpec(memory_space=pltpu.SMEM)] + [VM] * 7,
        out_specs=[VM] * 5,
        scratch_shapes=[pltpu.VMEM(s, d) for _, s, d in ACTS],
        compiler_params=pltpu.CompilerParams(vmem_limit_bytes=VMEM_BYTES),
    )(lens, mol[0], og[0], sp, bi.astype(F32)[None], w1, wi, wu.reshape(16, 4, 48, D))
    rs = lambda g: lax.psum_scatter(g.astype(F32), a, scatter_dimension=0, tiled=True)
    gu = rs(G[0:4].transpose(1, 0, 2, 3).reshape(FF, D))
    gi = rs(G[4:8].reshape(4, D, D).transpose(1, 0, 2).reshape(D, FF))
    g1 = G[8:12].reshape(2, 2, D, 2, 384).transpose(0, 3, 2, 1, 4).reshape(4, D, D)
    w = [rs(g1[k]) for k in range(4)]
    s = [rs(sg[k]) for k in range(8)]
    hist = pl.pallas_call(
        histogram, out_shape=S((2, 16, 32, 128), F32), in_specs=[VM], out_specs=VM
    )(ids)
    cnt = lax.psum(hist, a).reshape(128, 8, 128).transpose(1, 0, 2).reshape(8, BUCKETS).astype(I32)
    return (out[None], ing[None], s[0], s[1], w[0], s[2], w[1], w[2], s[3], w[3], s[4], s[5], s[6], gi, rs(sgi[0]), gu, s[7], cnt)


def solution(mesh):
    a = ("dp", "fsdp")
    r, r2, r3 = P(a), P(a, None), P(a, None, None)
    in_specs = (r3, r, P(None, a), r3, r, r, r2, r, r2, r2, r, r2, r, r, r, r2, r, r2, r)
    out_specs = (r3, r3, r, r, r2, r, r2, r2, r, r2, r, r, r, r2, r, r2, r, P())
    body = local if dict(mesh.shape) == {"dp": 4, "fsdp": 8} else plain
    return jax.shard_map(body, mesh=mesh, in_specs=in_specs, out_specs=out_specs, check_vma=False)
```
